32 devices in a mesh: seq: 8 (over y, x, core), ep: 4 (over z).
Axes of the slice: x: 2, y: 2, z: 4, core: 2. Of those that a mesh axis runs over, the one named last changes fastest.
Arguments:
- activations: bfloat16 [4096, 2880], P(('seq', 'ep')), may hold values from -6 to 6
- attn_gain: float32 [2880], replicated, may hold values from 0.1 to 1.9
- query_weight: bfloat16 [2880, 4096], P('seq', 'ep')
- key_weight: bfloat16 [2880, 512], P('seq', 'ep')
- value_weight: bfloat16 [2880, 512], P('seq', 'ep'), may hold values from -0.109375 to 0.109375
- output_weight: bfloat16 [4096, 2880], P('ep', 'seq'), may hold values from -0.375 to 0.375
- sink_logits: float32 [64], P('ep'), may hold values from 0 to 5
- mlp_gain: float32 [2880], replicated, may hold values from 0.1 to 1.9
- expert_ids: int32 [4096, 4], P(('seq', 'ep')), may hold values from 0 to 31, all different within a row; in each aligned block of 128 rows (0 to 127, 128 to 255, ...) at most 24 rows name the same one
- expert_gates: float32 [4096, 4], P(('seq', 'ep')), may hold values from 0.1 to 1
- expert_in: bfloat16 [32, 2880, 2880], P(('seq', 'ep')), may hold values from -0.109375 to 0.109375
- expert_out: bfloat16 [32, 1440, 2880], P(('seq', 'ep')), may hold values from -0.15625 to 0.15625
Outputs:
- layer_out: bfloat16 [4096, 2880], P(('seq', 'ep'))
The draws below stay inside these ranges and needn't reach their ends.
Inputs may be any that keep to these rules, and one draw needn't show every extreme that they name: `expert_ids`: in each aligned block of 128 rows (the rows of one device) no expert is named by more than 24 rows; in some blocks one expert is named by exactly 24 rows.
All inputs are finite; a program needn't handle non-finite values.
Results may differ from the reference program's by a relative error of at most 0.014.
The reference program's roundings to bfloat16 on the way count: a program that leaves them out, or rounds other values in their place, can miss the bound.
Values may be sent and summed in bfloat16 or wider, within the bound.
A program may use at most 128 MiB of HBM per device.

```python
import math
import jax
import jax.numpy as jnp
import numpy as np
from jax import lax

D = 2880
QH = 64
KVH = 8
HD = 64
FFW = 1440
TOPK = 4
WIN = 128
TOK_DEV = 512
EXPERTS = 32
TOKENS = 4096
MOE_TOK = 128
CAP = 24
N_EP = 4


def draw_activations(key, part):
    first_key = jax.random.fold_in(jax.random.fold_in(key, 3), 0)
    result = jnp.clip(jax.random.normal(first_key, (TOKENS, D), jnp.float32), -6.0, 6.0)
    return result.astype(jnp.bfloat16)


def attention_pair(key):
    first_key, second_key = jax.random.split(jax.random.fold_in(key, 11), 2)
    scale_in = D ** (-0.5)
    query_mat = jnp.clip(jax.random.normal(first_key, (D, QH * HD), jnp.float32), -6.0, 6.0) * scale_in
    key_mat = jnp.clip(jax.random.normal(second_key, (D, KVH * HD), jnp.float32), -6.0, 6.0) * scale_in
    return (query_mat, key_mat)


def draw_query_weight(key, part):
    return attention_pair(key)[0].astype(jnp.bfloat16)


def draw_key_weight(key, part):
    return attention_pair(key)[1].astype(jnp.bfloat16)


def levels(own_key, dims, shards, smallest, high):
    gain, own = 1.0, jax.random.fold_in(own_key, 6)
    for axis_at, shards_of in shards:
        heights = jnp.exp(jax.random.uniform(jax.random.fold_in(own, axis_at), (shards_of,), jnp.float32, smallest / len(shards), high / len(shards)))
        gain = gain * jnp.repeat(heights, dims[axis_at] // shards_of).reshape([-1 if axis == axis_at else 1 for axis in range(len(dims))])
    return gain


def deal_out(stream_key, own, number, rows, count, top, reach, slope):
    order = jax.random.permutation(stream_key, count)
    crowded, usual = load_shares(count, rows * top, reach, slope, True), load_shares(count, rows * top, reach, slope, False)
    places = jnp.arange(count)

    def named(sizes, turn):
        used = int((sizes > 0).sum())
        fixed = max(1, used // 4)
        passed = fixed + (places - fixed + turn * (used - fixed)) % max(1, count - fixed)
        return jnp.zeros((count,), jnp.int32).at[order[jnp.where(places < fixed, places, passed)]].set(jnp.asarray(sizes, jnp.int32))

    sizes = jnp.where(number % 4 == 0, named(crowded, number // 4), named(usual, number - number // 4 - 1))
    mixed = jax.random.permutation(jax.random.fold_in(own, 3), count)
    source_of, receiver = mixed[0:count // 2 * 2:2], mixed[1:count // 2 * 2:2]
    room = jnp.minimum(sizes[source_of] - 1, reach - sizes[receiver]) // 2
    room = jnp.where((source_of == order[0]) | (receiver == order[0]) | (sizes[receiver] == 0), 0, jnp.maximum(room, 0))
    passed = jax.random.randint(jax.random.fold_in(own, 4), (count // 2,), 0, 1 << 20) % (room + 1)
    sizes = sizes.at[source_of].add(-passed).at[receiver].add(passed)
    members = jnp.searchsorted(jnp.cumsum(sizes), jnp.arange(rows * top), side="right").astype(jnp.int32)
    table = members.reshape(top, rows).T
    table = table[jax.random.permutation(jax.random.fold_in(own, 1), rows)]
    turn = jax.random.randint(jax.random.fold_in(own, 2), (rows, 1), 0, top)
    return jnp.take_along_axis(table, (jnp.arange(top)[None, :] + turn) % top, axis=1)


def load_shares(amount, total, reach, slope, full):
    portions = [(1 << 20) // math.isqrt(standing ** slope) + 1 for standing in range(1, amount + 1)]
    largest = reach if full else min(reach, max(-(-total // amount), total * portions[0] // sum(portions)))
    least = 1 if total - largest >= amount - 1 else 0
    counts, spare = [largest] + [least] * (amount - 1), total - largest - least * (amount - 1)
    while spare > 0:
        movable = [i for i in range(1, amount) if counts[i] < largest] or [i for i in range(1, amount) if counts[i] < reach]
        pool, budget = sum([portions[i] for i in movable]), spare
        for i in movable:
            extra = min(reach - counts[i], max(1, budget * portions[i] // pool), spare)
            counts[i] = counts[i] + extra
            spare = spare - extra
    return np.array(counts)


def normal_values(rng, shape, deviation, bound, shards=(), held_as=jnp.bfloat16):
    values = deviation * jax.random.normal(rng, shape, jnp.float32)
    if shards:
        values = values * levels(rng, shape, shards, -0.22, 0.18)
    return jnp.clip(values, -bound, bound).astype(held_as)


def setup_inputs(seed: int = 0) -> dict:
    streams_of = jax.random.split(jax.random.key(seed), 13)
    activations = draw_activations(jax.random.fold_in(streams_of[12], 71), 0)
    attn_gain = jnp.clip(1.0 + 0.18 * jax.random.normal(streams_of[1], (D,), jnp.float32), 0.1, 1.9)
    query_weight = draw_query_weight(jax.random.fold_in(streams_of[12], 71), 0)
    key_weight = draw_key_weight(jax.random.fold_in(streams_of[12], 71), 0)
    value_weight = normal_values(streams_of[4], (D, KVH * HD), D ** -0.5, 0.109375, ((0, 8), (1, 4)))
    output_weight = normal_values(streams_of[5], (QH * HD, D), (QH * HD // 16) ** -0.5, 0.375, ((0, 4), (1, 8)))
    sink_logits = jnp.clip(5.0 * jax.random.uniform(streams_of[6], (QH,), jnp.float32) ** levels(streams_of[6], (QH,), ((0, 4),), -0.2, 0.2), 0.0, 5.0)
    mlp_gain = jnp.clip(1.0 + 0.18 * jax.random.normal(streams_of[7], (D,), jnp.float32), 0.1, 1.9)
    expert_ids_keys = jax.random.split(jax.random.fold_in(streams_of[8], 1), TOKENS // MOE_TOK)
    expert_ids_turns = jax.random.permutation(jax.random.fold_in(streams_of[8], 3), TOKENS // MOE_TOK)
    expert_ids = jax.vmap(lambda own, number: deal_out(jax.random.fold_in(streams_of[8], 2), own, number, MOE_TOK, EXPERTS, TOPK, CAP, 2))(expert_ids_keys, expert_ids_turns).reshape((TOKENS, TOPK))
    expert_gates = jnp.clip(0.1 + 0.9 * jax.random.uniform(streams_of[9], (TOKENS, TOPK), jnp.float32) ** levels(streams_of[9], (TOKENS, TOPK), ((0, 32),), -0.2, 0.2), 0.1, 1.0)
    expert_in = normal_values(streams_of[10], (EXPERTS, D, 2 * FFW), D ** -0.5, 0.109375, ((0, 32),))
    expert_out = normal_values(streams_of[11], (EXPERTS, FFW, D), FFW ** -0.5, 0.15625, ((0, 32),))
    return {"activations": activations, "attn_gain": attn_gain, "query_weight": query_weight, "key_weight": key_weight, "value_weight": value_weight, "output_weight": output_weight, "sink_logits": sink_logits, "mlp_gain": mlp_gain, "expert_ids": expert_ids, "expert_gates": expert_gates, "expert_in": expert_in, "expert_out": expert_out}


def normed(rows_f32, gain_vec):
    inv_rms = lax.rsqrt(lax.optimization_barrier(jnp.mean(rows_f32 * rows_f32, axis=-1, keepdims=True)) + 1e-05)
    return rows_f32 * inv_rms * gain_vec

def rotate(head_vals, positions):
    half_dim = head_vals.shape[-1] // 2
    inv_freq = 150000.0 ** (-jnp.arange(half_dim, dtype=jnp.float32) / half_dim)
    angles = positions[:, None] * inv_freq[None, :]
    cosines = jnp.cos(angles)[:, None, :]
    sines = jnp.sin(angles)[:, None, :]
    first = head_vals[..., :half_dim]
    second = head_vals[..., half_dim:]
    return jnp.concatenate([first * cosines - second * sines, second * cosines + first * sines], axis=-1)

def attend(queries, key_rows, val_rows, sink_grid, query_first, win_len):
    scores = jnp.einsum('qkgd,jkd->kgqj', queries.astype(jnp.float32), key_rows.astype(jnp.float32)) * 0.125
    q_pos = query_first + jnp.arange(queries.shape[0], dtype=jnp.int32)
    k_pos = query_first - win_len + jnp.arange(key_rows.shape[0], dtype=jnp.int32)
    offset = q_pos[:, None] - k_pos[None, :]
    allowed = (offset >= 0) & (offset < win_len) & (k_pos[None, :] >= 0)
    scores = jnp.where(allowed, scores, jnp.float32(-1e+30))
    peak_val = jnp.maximum(lax.optimization_barrier(jnp.max(scores, axis=-1)), sink_grid[:, :, None])
    exp_terms = jnp.exp(scores - peak_val[..., None])
    denominator = lax.optimization_barrier(jnp.sum(exp_terms, axis=-1)) + jnp.exp(sink_grid[:, :, None] - peak_val)
    weights = (exp_terms / denominator[..., None]).astype(jnp.bfloat16)
    mixed_vals = jnp.einsum('kgqj,jkd->qkgd', weights.astype(jnp.float32), val_rows.astype(jnp.float32))
    return mixed_vals.astype(jnp.bfloat16)

def run_expert(arrived, gate_up, down_proj):
    hidden_units = down_proj.shape[0]
    joined = jnp.dot(arrived, gate_up, preferred_element_type=jnp.float32)
    gate_part = joined[:, :hidden_units]
    up_part = joined[:, hidden_units:]
    activated = ((up_part + 1.0) * gate_part * jax.nn.sigmoid(1.702 * gate_part)).astype(jnp.bfloat16)
    return jnp.dot(activated, down_proj, preferred_element_type=jnp.float32).astype(jnp.bfloat16)

def reference(activations, attn_gain, query_weight, key_weight, value_weight, output_weight, sink_logits, mlp_gain, expert_ids, expert_gates, expert_in, expert_out):
    act_f32 = activations.astype(jnp.float32)
    normed_in = normed(act_f32, attn_gain).astype(jnp.bfloat16)
    q_lin = jnp.dot(normed_in, query_weight, preferred_element_type=jnp.float32)
    k_lin = jnp.dot(normed_in, key_weight, preferred_element_type=jnp.float32)
    v_lin = jnp.dot(normed_in, value_weight, preferred_element_type=jnp.float32)
    positions = jnp.arange(TOKENS, dtype=jnp.float32)
    group_size = QH // KVH
    queries = rotate(q_lin.reshape(TOKENS, QH, HD), positions).astype(jnp.bfloat16).reshape(TOKENS, KVH, group_size, HD)
    keys_rot = rotate(k_lin.reshape(TOKENS, KVH, HD), positions).astype(jnp.bfloat16)
    values_cast = v_lin.astype(jnp.bfloat16).reshape(TOKENS, KVH, HD)
    padding = jnp.zeros((WIN, KVH, HD), jnp.bfloat16)
    key_all = jnp.concatenate([padding, keys_rot], axis=0)
    val_all = jnp.concatenate([padding, values_cast], axis=0)
    block_len = min(TOK_DEV, 512)
    sink_grid = sink_logits.reshape(KVH, group_size)

    def one_block(block):
        row_first = block * block_len
        q_block = lax.dynamic_slice_in_dim(queries, row_first, block_len, 0)
        k_block = lax.dynamic_slice_in_dim(key_all, row_first, block_len + WIN, 0)
        v_block = lax.dynamic_slice_in_dim(val_all, row_first, block_len + WIN, 0)
        return attend(q_block, k_block, v_block, sink_grid, row_first, WIN)
    attended = lax.map(one_block, jnp.arange(TOKENS // block_len, dtype=jnp.int32)).reshape(TOKENS, QH * HD)
    head_cols = QH * HD // N_EP
    head_sum = jnp.zeros((TOKENS, D), jnp.float32)
    for group_index in range(N_EP):
        lower = group_index * head_cols
        partial_sum = jnp.dot(attended[:, lower:lower + head_cols], output_weight[lower:lower + head_cols], preferred_element_type=jnp.float32).astype(jnp.bfloat16)
        partial_sum = lax.optimization_barrier(partial_sum)
        head_sum = head_sum + partial_sum.astype(jnp.float32)
    mixed = act_f32 + head_sum
    mlp_in = normed(mixed, mlp_gain).astype(jnp.bfloat16)
    blocks = TOKENS // MOE_TOK
    per_block = MOE_TOK * TOPK
    flat_ids = expert_ids.reshape(blocks, per_block).astype(jnp.int32)
    one_hot = (flat_ids[:, :, None] == jnp.arange(EXPERTS, dtype=jnp.int32)[None, None, :]).astype(jnp.int32)
    ranks = lax.optimization_barrier(jnp.sum(one_hot * (jnp.cumsum(one_hot, axis=1) - 1), axis=-1)).astype(jnp.int32)
    block_ids = jnp.arange(blocks, dtype=jnp.int32)[:, None]
    slots = ((flat_ids * blocks + block_ids) * CAP + ranks).reshape(-1).astype(jnp.int32)
    token_ids = (jnp.arange(TOKENS * TOPK, dtype=jnp.int32) // TOPK).astype(jnp.int32)
    table = jnp.zeros((EXPERTS * blocks * CAP,), jnp.int32).at[slots].set(token_ids).reshape(EXPERTS, blocks * CAP)
    gate_table = jnp.zeros((EXPERTS * blocks * CAP,), jnp.float32).at[slots].set(expert_gates.reshape(-1)).reshape(EXPERTS, blocks * CAP)

    def visit(running, items):
        rows_at, gate_rows, gate_up, down_proj = items
        results = run_expert(mlp_in[rows_at], gate_up, down_proj)
        running = running.at[rows_at].add(gate_rows[:, None] * results.astype(jnp.float32))
        return (running, None)
    moe_sum, _ = lax.scan(visit, jnp.zeros((TOKENS, D), jnp.float32), (table, gate_table, expert_in, expert_out))
    return (mixed + moe_sum).astype(jnp.bfloat16)
```

```python
import functools

import jax
import jax.numpy as jnp
from jax import lax
from jax.experimental import pallas as pl
from jax.experimental.layout import Layout, with_layout_constraint
from jax.experimental.pallas import tpu as pltpu
from jax.sharding import PartitionSpec as P

MESH = pl.DeviceIdType.MESH

HD = 64
WIN = 128


def passed_along(x, axis, by):
    count = lax.axis_size(axis)
    pairs = [(i, i + by) for i in range(count) if 0 <= i + by < count]
    return lax.ppermute(x, axis, pairs)


def normed(rows_f32, gain_vec):
    inv_rms = lax.rsqrt(jnp.mean(rows_f32 * rows_f32, axis=-1, keepdims=True) + 1e-05)
    return rows_f32 * inv_rms * gain_vec


def rotate(head_vals, positions):
    half_dim = head_vals.shape[-1] // 2
    inv_freq = 150000.0 ** (-jnp.arange(half_dim, dtype=jnp.float32) / half_dim)
    angles = positions[:, None] * inv_freq[None, :]
    cosines = jnp.cos(angles)[:, None, :]
    sines = jnp.sin(angles)[:, None, :]
    first = head_vals[..., :half_dim]
    second = head_vals[..., half_dim:]
    return jnp.concatenate(
        [first * cosines - second * sines, second * cosines + first * sines], axis=-1
    )


def attend(queries, key_rows, val_rows, sink_grid, query_first, win_len):
    scores = (
        jnp.einsum("qkgd,jkd->kgqj", queries, key_rows, preferred_element_type=jnp.float32) * 0.125
    )
    q_pos = query_first + jnp.arange(queries.shape[0], dtype=jnp.int32)
    k_pos = query_first - win_len + jnp.arange(key_rows.shape[0], dtype=jnp.int32)
    offset = q_pos[:, None] - k_pos[None, :]
    allowed = (offset >= 0) & (offset < win_len) & (k_pos[None, :] >= 0)
    scores = jnp.where(allowed, scores, jnp.float32(-1e30))
    peak_val = jnp.maximum(jnp.max(scores, axis=-1), sink_grid[:, :, None])
    exp_terms = jnp.exp(scores - peak_val[..., None])
    denominator = jnp.sum(exp_terms, axis=-1) + jnp.exp(sink_grid[:, :, None] - peak_val)
    weights = (exp_terms / denominator[..., None]).astype(jnp.bfloat16)
    mixed_vals = jnp.einsum("kgqj,jkd->qkgd", weights, val_rows, preferred_element_type=jnp.float32)
    return mixed_vals.astype(jnp.bfloat16)


def remote(src, dst, send_sem, recv_sem, device):
    return pltpu.make_async_remote_copy(
        src_ref=src,
        dst_ref=dst,
        send_sem=send_sem,
        recv_sem=recv_sem,
        device_id=device,
        device_id_type=MESH,
    )


def gather_kernel(n_seq, n_ep, n_line, n_plane, *refs):
    total = n_line + n_plane
    ins, outs, bufs = refs[:total], refs[total : 2 * total], refs[2 * total : 3 * total]
    own_sem, line_send, line_recv, plane_send, plane_recv, fwd_send = refs[3 * total :]
    seq, ep = lax.axis_index("seq"), lax.axis_index("ep")
    chips = n_seq // 2
    chip, core = seq // 2, seq % 2
    partner = chip * 2 + 1 - core

    barrier = pltpu.get_barrier_semaphore()

    @pl.when(ep > 0)
    def _():
        pl.semaphore_signal(barrier, inc=1, device_id=(seq, ep - 1), device_id_type=MESH)

    @pl.when(ep < n_ep - 1)
    def _():
        pl.semaphore_signal(barrier, inc=1, device_id=(seq, ep + 1), device_id_type=MESH)

    for d in range(1, chips):
        peer = lax.rem(chip + d, chips) * 2 + core
        pl.semaphore_signal(barrier, inc=1, device_id=(peer, ep), device_id_type=MESH)
    pl.semaphore_signal(barrier, inc=1, device_id=(partner, ep), device_id_type=MESH)
    neighbours = (ep > 0).astype(jnp.int32) + (ep < n_ep - 1).astype(jnp.int32)
    pl.semaphore_wait(barrier, chips + neighbours)

    def line_copies(step, which, act):
        for i in which:
            left_src, right_src = ep - step, ep + step

            @pl.when((left_src >= 0) & (ep < n_ep - 1))
            def _():
                src = ins[i] if step == 0 else outs[i].at[left_src]
                act(
                    remote(
                        src,
                        outs[i].at[left_src],
                        line_send.at[i, 0, step],
                        line_recv.at[i, left_src],
                        (seq, ep + 1),
                    )
                )

            @pl.when((right_src < n_ep) & (ep > 0))
            def _():
                src = ins[i] if step == 0 else outs[i].at[right_src]
                act(
                    remote(
                        src,
                        outs[i].at[right_src],
                        line_send.at[i, 1, step],
                        line_recv.at[i, right_src],
                        (seq, ep - 1),
                    )
                )

    def line_arrived(step, which):
        for i in which:
            for src in (ep - step, ep + step):

                @pl.when((src >= 0) & (src < n_ep))
                def _():
                    remote(
                        ins[i],
                        outs[i].at[src],
                        line_send.at[i, 0, 0],
                        line_recv.at[i, src],
                        (seq, ep),
                    ).wait_recv()

    def plane_copy(i, d):
        peer = lax.rem(chip + d, chips) * 2 + core
        if d == 0:
            peer = partner
        return remote(
            ins[n_line + i],
            outs[n_line + i].at[seq],
            plane_send.at[i, d],
            plane_recv.at[i, seq],
            (peer, ep),
        )

    def fwd_copy(i, d):
        src = lax.rem(chip + d, chips) * 2 + core
        return remote(
            outs[n_line + i].at[src],
            outs[n_line + i].at[src],
            fwd_send.at[i, d],
            plane_recv.at[i, src],
            (partner, ep),
        )

    def plane_arrived(i, src):
        remote(
            ins[n_line + i],
            outs[n_line + i].at[src],
            plane_send.at[i, 0],
            plane_recv.at[i, src],
            (partner, ep),
        ).wait_recv()

    every = range(n_line)
    line_copies(0, every, lambda c: c.start())
    for i in range(n_plane):
        for d in range(chips):
            plane_copy(i, d).start()
    for i in range(total):
        pltpu.make_async_copy(ins[i], bufs[i], own_sem.at[i]).start()
    for i in range(total):
        pltpu.make_async_copy(ins[i], bufs[i], own_sem.at[i]).wait()
        mine = outs[i].at[ep if i < n_line else seq]
        pltpu.make_async_copy(bufs[i], mine, own_sem.at[i]).start()
    for step in range(1, n_ep - 1):
        line_arrived(step, every)
        line_copies(step, every, lambda c: c.start())
    for i in range(n_plane):
        for d in range(1, chips):
            plane_arrived(i, lax.rem(chip + d, chips) * 2 + core)
            fwd_copy(i, d).start()
    line_arrived(n_ep - 1, every)
    for i in range(n_plane):
        for d in range(chips):
            plane_arrived(i, lax.rem(chip + d, chips) * 2 + 1 - core)
    for i in range(total):
        mine = outs[i].at[ep if i < n_line else seq]
        pltpu.make_async_copy(bufs[i], mine, own_sem.at[i]).wait()
    for step in range(n_ep - 1):
        line_copies(step, every, lambda c: c.wait_send())
    for i in range(n_plane):
        for d in range(chips):
            plane_copy(i, d).wait_send()
        for d in range(1, chips):
            fwd_copy(i, d).wait_send()


def gathered(line, plane):
    n_seq, n_ep = lax.axis_size("seq"), lax.axis_size("ep")
    arrays = tuple(line) + tuple(plane)
    n_line, n_plane, chips = len(line), len(plane), n_seq // 2
    counts = [n_ep] * n_line + [n_seq] * n_plane
    anywhere = pl.BlockSpec(memory_space=pl.ANY)
    sem = pltpu.SemaphoreType.DMA
    return pl.pallas_call(
        functools.partial(gather_kernel, n_seq, n_ep, n_line, n_plane),
        out_shape=[jax.ShapeDtypeStruct((c,) + a.shape, a.dtype) for c, a in zip(counts, arrays)],
        in_specs=[anywhere] * len(arrays),
        out_specs=[anywhere] * len(arrays),
        scratch_shapes=[pltpu.VMEM(a.shape, a.dtype) for a in arrays]
        + [
            sem((len(arrays),)),
            sem((n_line, 2, n_ep)),
            sem((n_line, n_ep)),
            sem((n_plane, chips)),
            sem((n_plane, n_seq)),
            sem((n_plane, chips)),
        ],
        compiler_params=pltpu.CompilerParams(
            collective_id=0, has_side_effects=True, vmem_limit_bytes=16 << 20
        ),
        name="gather",
    )(*arrays)


def signal_all(barrier, n_seq, n_ep, seq, ep, line):
    for d in range(1, n_seq):
        pl.semaphore_signal(
            barrier, inc=1, device_id=(lax.rem(seq + d, n_seq), ep), device_id_type=MESH
        )
    count = jnp.int32(n_seq - 1)
    for d in line:
        there = (ep + d >= 0) & (ep + d < n_ep)

        @pl.when(there)
        def _():
            pl.semaphore_signal(barrier, inc=1, device_id=(seq, ep + d), device_id_type=MESH)

        count = count + there.astype(jnp.int32)
    pl.semaphore_wait(barrier, count)


def column_chunks(width, most=1024):
    return [(c, min(most, width - c)) for c in range(0, width, most)]


def moe_kernel(
    n_seq,
    n_ep,
    cap,
    x_ref,
    pick_ref,
    gate_ref,
    mixed_ref,
    win_hbm,
    wout_hbm,
    out_ref,
    held,
    staged,
    arrived,
    back,
    sums,
    mine,
    taken,
    joined,
    act,
    w_in,
    w_out,
    weight_sem,
    line_send,
    line_recv,
    send,
    recv,
    own,
    back_send,
    back_recv,
    back_own,
    sum_send,
    sum_recv,
):
    seq, ep = lax.axis_index("seq"), lax.axis_index("ep")
    rows, width = mixed_ref.shape
    slots = n_seq * cap
    hidden = wout_hbm.shape[0]
    far = [d for d in range(1 - n_ep, n_ep) if d != 0]
    in_copy = pltpu.make_async_copy(win_hbm, w_in, weight_sem.at[0])
    out_copy = pltpu.make_async_copy(wout_hbm, w_out, weight_sem.at[1])
    in_copy.start()
    out_copy.start()
    signal_all(pltpu.get_barrier_semaphore(), n_seq, n_ep, seq, ep, far)

    def spread(buffer, c, size, value):
        for s in range(n_seq):
            buffer[s, :, pl.ds(c, size)] = value[s * cap : (s + 1) * cap].astype(jnp.bfloat16)

    def together(buffer, c, size, first, count):
        slabs = [buffer[first + s, :, c : c + size].astype(jnp.float32) for s in range(count)]
        return jnp.concatenate(slabs, axis=0).astype(jnp.bfloat16)

    def relay(step, src, away, act_on):
        @pl.when((src >= 0) & (src < n_ep) & (ep + away >= 0) & (ep + away < n_ep))
        def _():
            act_on(
                remote(
                    x_ref if step == 0 else held.at[src],
                    held.at[src],
                    line_send.at[(away + 1) // 2, step],
                    line_recv.at[src],
                    (seq, ep + away),
                )
            )

    def part(src, d):
        peer = lax.rem(seq + d, n_seq)
        return remote(
            staged.at[src, peer],
            arrived.at[src, seq],
            send.at[src, d],
            recv.at[src, seq],
            (peer, ep),
        )

    def own_part(src):
        return pltpu.make_async_copy(
            staged.at[src, seq], arrived.at[src, seq], own.at[src]
        )

    def back_part(src, d):
        peer = lax.rem(seq + d, n_seq)
        return remote(
            staged.at[src, peer],
            back.at[src, seq],
            back_send.at[src, d],
            back_recv.at[src, seq],
            (peer, ep),
        )

    def back_own_part(src):
        return pltpu.make_async_copy(
            staged.at[src, seq], back.at[src, seq], back_own.at[src]
        )

    def sum_copy(at):
        return remote(held.at[at], sums.at[ep], sum_send.at[at], sum_recv.at[ep], (seq, at))

    def each(d, act_on):
        at = ep + d

        @pl.when((at >= 0) & (at < n_ep))
        def _():
            act_on(at)

    def hand_out(src, rows_ref):
        for c, size in column_chunks(width):
            picked = jnp.dot(
                pick_ref[src], rows_ref[:, c : c + size], preferred_element_type=jnp.float32
            )
            spread(staged.at[src], c, size, picked)
        for d in range(1, n_seq):
            part(src, d).start()
        own_part(src).start()

    def expert(src):
        own_part(src).wait()
        for d in range(1, n_seq):
            peer = lax.rem(seq + d, n_seq)
            remote(
                staged.at[src, seq],
                arrived.at[src, peer],
                send.at[src, 0],
                recv.at[src, peer],
                (peer, ep),
            ).wait_recv()

        group = n_seq if slots % 16 else 2
        for s in range(0, n_seq, group):
            taken[s * cap : (s + group) * cap, :] = together(arrived.at[src], 0, width, s, group)

        def up_columns(c, size):
            joined[:, pl.ds(c, size)] = jnp.dot(
                taken[...], w_in[:, pl.ds(c, size)], preferred_element_type=jnp.float32
            )

        @pl.loop(0, width // 512)
        def _(i):
            up_columns(pl.multiple_of(i * 512, 512), 512)

        if width % 512:
            up_columns(width // 512 * 512, width % 512)

        @pl.loop(0, slots // 16)
        def _(i):
            r = pl.ds(pl.multiple_of(i * 16, 16), 16)
            gate = joined[r, 0:hidden]
            up = joined[r, hidden : 2 * hidden]
            act[r, :] = ((up + 1.0) * gate * jax.nn.sigmoid(1.702 * gate)).astype(jnp.bfloat16)

        for d in range(1, n_seq):
            part(src, d).wait_send()

        def down_columns(c, size):
            value = jnp.dot(
                act[...], w_out[:, pl.ds(c, size)], preferred_element_type=jnp.float32
            )
            spread(staged.at[src], c, size, value)

        @pl.loop(0, width // 512)
        def _(i):
            down_columns(pl.multiple_of(i * 512, 512), 512)

        if width % 512:
            down_columns(width // 512 * 512, width % 512)
        for d in range(1, n_seq):
            back_part(src, d).start()
        back_own_part(src).start()

    def gather_up(at, finish):
        back_own_part(at).wait()
        for d in range(1, n_seq):
            peer = lax.rem(seq + d, n_seq)
            remote(
                staged.at[at, seq],
                back.at[at, peer],
                back_send.at[at, 0],
                back_recv.at[at, peer],
                (peer, ep),
            ).wait_recv()
        for c, size in column_chunks(width):
            results = together(back.at[at], c, size, 0, n_seq)
            three = jnp.dot(gate_ref[at], results, preferred_element_type=jnp.float32)
            finish(c, size, three[:rows] + three[rows : 2 * rows] + three[2 * rows :])

    def pass_on(step, way):
        at = ep + way * step

        @pl.when((at >= 0) & (at < n_ep))
        def _():
            relay(step, at, -way, lambda c: c.wait_send())

            def finish(c, size, value):
                held[at, :, c : c + size] = value.astype(jnp.bfloat16)

            gather_up(at, finish)
            sum_copy(at).start()

    relay(0, ep, 1, lambda c: c.start())
    relay(0, ep, -1, lambda c: c.start())
    hand_out(ep, x_ref)
    for step in range(1, n_ep):
        for way in (1, -1):
            src = ep - way * step

            @pl.when((src >= 0) & (src < n_ep))
            def _():
                remote(
                    x_ref, held.at[src], line_send.at[0, 0], line_recv.at[src], (seq, ep)
                ).wait_recv()

            relay(step, src, way, lambda c: c.start())
        for way in (1, -1):
            each(-way * step, lambda at: hand_out(at, held.at[at]))
        if step == 1:
            in_copy.wait()
            out_copy.wait()
            expert(ep)
        else:
            for way in (1, -1):
                each(-way * (step - 1), expert)
            if step > 2:
                for way in (1, -1):
                    pass_on(step - 2, way)
    for way in (1, -1):
        each(-way * (n_ep - 1), expert)
    if n_ep > 2:
        for way in (1, -1):
            pass_on(n_ep - 2, way)

    def keep(c, size, value):
        mine[:, c : c + size] = mixed_ref[:, c : c + size] + value

    gather_up(ep, keep)
    for way in (1, -1):
        pass_on(n_ep - 1, way)

    def add(at):
        remote(held.at[at], sums.at[at], sum_send.at[at], sum_recv.at[at], (seq, at)).wait_recv()
        for c, size in column_chunks(width):
            mine[:, c : c + size] += sums[at, :, c : c + size].astype(jnp.float32)

    order = sorted(far, key=lambda d: (abs(d), d))
    for d in order:
        each(d, add)
    for c, size in column_chunks(width):
        out_ref[:, c : c + size] = mine[:, c : c + size].astype(jnp.bfloat16)
    for d in order:
        each(d, lambda at: sum_copy(at).wait_send())
    for way in (1, -1):
        relay(0, ep, way, lambda c: c.wait_send())
    for src in range(n_ep):
        for d in range(1, n_seq):
            back_part(src, d).wait_send()


def mixture(rows_in, picks, gates, mixed, w_in, w_out, cap):
    n_seq, n_ep = lax.axis_size("seq"), lax.axis_size("ep")
    rows, width = mixed.shape
    hidden = w_out.shape[0]
    slots = n_seq * cap
    sem = pltpu.SemaphoreType.DMA
    vmem = pl.BlockSpec(memory_space=pltpu.VMEM)
    anywhere = pl.BlockSpec(memory_space=pl.ANY)
    return pl.pallas_call(
        functools.partial(moe_kernel, n_seq, n_ep, cap),
        out_shape=jax.ShapeDtypeStruct((rows, width), jnp.bfloat16),
        in_specs=[vmem, vmem, vmem, vmem, anywhere, anywhere],
        out_specs=vmem,
        scratch_shapes=[
            pltpu.VMEM((n_ep, rows, width), jnp.bfloat16),
            pltpu.VMEM((n_ep, n_seq, cap, width), jnp.bfloat16),
            pltpu.VMEM((n_ep, n_seq, cap, width), jnp.bfloat16),
            pltpu.VMEM((n_ep, n_seq, cap, width), jnp.bfloat16),
            pltpu.VMEM((n_ep, rows, width), jnp.bfloat16),
            pltpu.VMEM((rows, width), jnp.float32),
            pltpu.VMEM((slots, width), jnp.bfloat16),
            pltpu.VMEM((slots, width), jnp.float32),
            pltpu.VMEM((slots, hidden), jnp.bfloat16),
            pltpu.VMEM(w_in.shape, jnp.bfloat16),
            pltpu.VMEM(w_out.shape, jnp.bfloat16),
            sem((2,)),
            sem((2, n_ep)),
            sem((n_ep,)),
            sem((n_ep, n_seq)),
            sem((n_ep, n_seq)),
            sem((n_ep,)),
            sem((n_ep, n_seq)),
            sem((n_ep, n_seq)),
            sem((n_ep,)),
            sem((n_ep,)),
            sem((n_ep,)),
        ],
        compiler_params=pltpu.CompilerParams(
            collective_id=1, has_side_effects=True, vmem_limit_bytes=64000 << 10
        ),
        name="mixture",
    )(rows_in, picks, gates, mixed, w_in, w_out)


def slot_of(ids, capacity):
    count = ids.size
    flat = ids.reshape(-1)
    earlier = jnp.arange(count)[:, None] > jnp.arange(count)[None, :]
    same = (flat[:, None] == flat[None, :]) & earlier
    ranks = jnp.sum(same.astype(jnp.int32), axis=1)
    return (flat * capacity + ranks).reshape(ids.shape)


def three_parts(x):
    high = lax.reduce_precision(x, 8, 7)
    rest = x - high
    middle = lax.reduce_precision(rest, 8, 7)
    return high.astype(jnp.bfloat16), middle.astype(jnp.bfloat16), (rest - middle).astype(jnp.bfloat16)


def by_rows(x):
    return with_layout_constraint(x, Layout(tuple(range(x.ndim))))


def body(
    activations,
    attn_gain,
    query_weight,
    key_weight,
    value_weight,
    output_weight,
    sink_logits,
    mlp_gain,
    expert_ids,
    expert_gates,
    expert_in,
    expert_out,
):
    own_rows = activations.shape[0]
    width_dim = activations.shape[1]
    seq_count = lax.axis_size("seq")
    ep_count = lax.axis_size("ep")
    tok_rows = own_rows * ep_count
    act_f32 = activations.astype(jnp.float32)
    normed_own = normed(act_f32, attn_gain).astype(jnp.bfloat16)
    q_cols = query_weight.shape[1]
    kv_cols = key_weight.shape[1]
    experts_all = seq_count * ep_count
    top_k = expert_ids.shape[1]
    capacity = max(2, 3 * own_rows * top_k // (2 * experts_all))
    capacity = -(-capacity // 8) * 8
    out_rows = lax.all_gather(output_weight.T, "seq", axis=0, tiled=True)
    (normed_all, line_slots, line_gates, *shard_rows) = gathered(
        (normed_own, slot_of(expert_ids, capacity).T, expert_gates.T),
        (query_weight, key_weight, value_weight),
    )
    normed_all = normed_all.reshape(tok_rows, width_dim)
    shard_rows = [rows.reshape(width_dim, -1) for rows in shard_rows]
    q_lin, k_lin, v_lin = tuple(
        (
            jnp.dot(normed_all, weight_rows, preferred_element_type=jnp.float32)
            for weight_rows in shard_rows
        )
    )
    q_lin, k_lin = by_rows(q_lin), by_rows(k_lin)
    first_pos = lax.axis_index("seq") * tok_rows
    positions = (first_pos + jnp.arange(tok_rows, dtype=jnp.int32)).astype(jnp.float32)
    q_heads = q_cols // HD
    kv_heads = kv_cols // HD
    group_size = q_heads // kv_heads
    queries = (
        rotate(q_lin.reshape(tok_rows, q_heads, HD), positions)
        .astype(jnp.bfloat16)
        .reshape(tok_rows, kv_heads, group_size, HD)
    )
    keys_rot = (
        rotate(k_lin.reshape(tok_rows, kv_heads, HD), positions)
        .astype(jnp.bfloat16)
        .reshape(tok_rows, kv_cols)
    )
    values_cast = v_lin.astype(jnp.bfloat16)
    prev_keys, prev_values = passed_along(
        (keys_rot[tok_rows - WIN :], values_cast[tok_rows - WIN :]), "seq", 1
    )
    key_all = jnp.concatenate([prev_keys, keys_rot], axis=0).reshape(WIN + tok_rows, kv_heads, HD)
    val_all = jnp.concatenate([prev_values, values_cast], axis=0).reshape(
        WIN + tok_rows, kv_heads, HD
    )
    block_len = min(tok_rows, 512)
    sink_grid = sink_logits.reshape(kv_heads, group_size)

    def one_block(block):
        row_first = block * block_len
        return attend(queries, key_all, val_all, sink_grid, first_pos + row_first, WIN)

    attended = lax.map(one_block, jnp.arange(tok_rows // block_len, dtype=jnp.int32)).reshape(
        tok_rows, q_cols
    )
    head_partial = lax.dot_general(
        attended, out_rows, (((1,), (1,)), ((), ())), preferred_element_type=jnp.float32
    ).astype(jnp.bfloat16)
    head_sum = lax.psum_scatter(
        by_rows(head_partial), "ep", scatter_dimension=0, tiled=True
    ).astype(jnp.float32)
    mixed = act_f32 + head_sum
    mlp_in = normed(mixed, mlp_gain).astype(jnp.bfloat16)
    plane_rows = seq_count * capacity
    place = jnp.arange(plane_rows, dtype=jnp.int32)
    first_slots = (place // capacity * ep_count + lax.axis_index("ep")) * capacity
    plane_slots = first_slots + place % capacity
    picks = sum(
        (line_slots[:, k, None, :] == plane_slots[None, :, None]).astype(jnp.bfloat16)
        for k in range(top_k)
    )
    gate_at = sum(
        jnp.where(
            line_slots[:, k, :, None] == plane_slots[None, None, :],
            line_gates[:, k, :, None],
            0.0,
        )
        for k in range(top_k)
    )
    gate_parts = jnp.concatenate(three_parts(gate_at), axis=1)
    return mixture(
        mlp_in, picks, gate_parts, mixed, expert_in[0], expert_out[0], capacity
    )


def solution(mesh):
    return jax.shard_map(
        body,
        mesh=mesh,
        in_specs=(
            P(("seq", "ep"), None),
            P(),
            P("seq", "ep"),
            P("seq", "ep"),
            P("seq", "ep"),
            P("ep", "seq"),
            P("ep"),
            P(),
            P(("seq", "ep"), None),
            P(("seq", "ep"), None),
            P(("seq", "ep"), None, None),
            P(("seq", "ep"), None, None),
        ),
        out_specs=P(("seq", "ep"), None),
        check_vma=False,
    )
```

```python
import functools

import jax
import jax.numpy as jnp
from jax import lax
from jax.experimental import pallas as pl
from jax.experimental.layout import Layout, with_layout_constraint
from jax.experimental.pallas import tpu as pltpu
from jax.sharding import PartitionSpec as P

MESH = pl.DeviceIdType.MESH

HD = 64
WIN = 128


def passed_along(x, axis, by):
    count = lax.axis_size(axis)
    pairs = [(i, i + by) for i in range(count) if 0 <= i + by < count]
    return lax.ppermute(x, axis, pairs)


def normed(rows_f32, gain_vec):
    inv_rms = lax.rsqrt(jnp.mean(rows_f32 * rows_f32, axis=-1, keepdims=True) + 1e-05)
    return rows_f32 * inv_rms * gain_vec


def rotate(head_vals, positions):
    half_dim = head_vals.shape[-1] // 2
    inv_freq = 150000.0 ** (-jnp.arange(half_dim, dtype=jnp.float32) / half_dim)
    angles = positions[:, None] * inv_freq[None, :]
    cosines = jnp.cos(angles)[:, None, :]
    sines = jnp.sin(angles)[:, None, :]
    first = head_vals[..., :half_dim]
    second = head_vals[..., half_dim:]
    return jnp.concatenate(
        [first * cosines - second * sines, second * cosines + first * sines], axis=-1
    )


def attend(queries, key_rows, val_rows, sink_grid, query_first, win_len):
    scores = (
        jnp.einsum("qkgd,jkd->kgqj", queries, key_rows, preferred_element_type=jnp.float32) * 0.125
    )
    q_pos = query_first + jnp.arange(queries.shape[0], dtype=jnp.int32)
    k_pos = query_first - win_len + jnp.arange(key_rows.shape[0], dtype=jnp.int32)
    offset = q_pos[:, None] - k_pos[None, :]
    allowed = (offset >= 0) & (offset < win_len) & (k_pos[None, :] >= 0)
    scores = jnp.where(allowed, scores, jnp.float32(-1e30))
    peak_val = jnp.maximum(jnp.max(scores, axis=-1), sink_grid[:, :, None])
    exp_terms = jnp.exp(scores - peak_val[..., None])
    denominator = jnp.sum(exp_terms, axis=-1) + jnp.exp(sink_grid[:, :, None] - peak_val)
    weights = (exp_terms / denominator[..., None]).astype(jnp.bfloat16)
    mixed_vals = jnp.einsum("kgqj,jkd->qkgd", weights, val_rows, preferred_element_type=jnp.float32)
    return mixed_vals.astype(jnp.bfloat16)


def remote(src, dst, send_sem, recv_sem, device):
    return pltpu.make_async_remote_copy(
        src_ref=src,
        dst_ref=dst,
        send_sem=send_sem,
        recv_sem=recv_sem,
        device_id=device,
        device_id_type=MESH,
    )


def gather_kernel(n_seq, n_ep, n_line, n_plane, *refs):
    total = n_line + n_plane
    ins, outs, bufs = refs[:total], refs[total : 2 * total], refs[2 * total : 3 * total]
    own_sem, line_send, line_recv, plane_send, plane_recv, fwd_send = refs[3 * total :]
    seq, ep = lax.axis_index("seq"), lax.axis_index("ep")
    chips = n_seq // 2
    chip, core = seq // 2, seq % 2
    partner = chip * 2 + 1 - core

    barrier = pltpu.get_barrier_semaphore()

    @pl.when(ep > 0)
    def _():
        pl.semaphore_signal(barrier, inc=1, device_id=(seq, ep - 1), device_id_type=MESH)

    @pl.when(ep < n_ep - 1)
    def _():
        pl.semaphore_signal(barrier, inc=1, device_id=(seq, ep + 1), device_id_type=MESH)

    for d in range(1, chips):
        peer = lax.rem(chip + d, chips) * 2 + core
        pl.semaphore_signal(barrier, inc=1, device_id=(peer, ep), device_id_type=MESH)
    pl.semaphore_signal(barrier, inc=1, device_id=(partner, ep), device_id_type=MESH)
    neighbours = (ep > 0).astype(jnp.int32) + (ep < n_ep - 1).astype(jnp.int32)
    pl.semaphore_wait(barrier, chips + neighbours)

    def line_copies(step, which, act):
        for i in which:
            left_src, right_src = ep - step, ep + step

            @pl.when((left_src >= 0) & (ep < n_ep - 1))
            def _():
                src = ins[i] if step == 0 else outs[i].at[left_src]
                act(
                    remote(
                        src,
                        outs[i].at[left_src],
                        line_send.at[i, 0, step],
                        line_recv.at[i, left_src],
                        (seq, ep + 1),
                    )
                )

            @pl.when((right_src < n_ep) & (ep > 0))
            def _():
                src = ins[i] if step == 0 else outs[i].at[right_src]
                act(
                    remote(
                        src,
                        outs[i].at[right_src],
                        line_send.at[i, 1, step],
                        line_recv.at[i, right_src],
                        (seq, ep - 1),
                    )
                )

    def line_arrived(step, which):
        for i in which:
            for src in (ep - step, ep + step):

                @pl.when((src >= 0) & (src < n_ep))
                def _():
                    remote(
                        ins[i],
                        outs[i].at[src],
                        line_send.at[i, 0, 0],
                        line_recv.at[i, src],
                        (seq, ep),
                    ).wait_recv()

    def plane_copy(i, d):
        peer = lax.rem(chip + d, chips) * 2 + core
        if d == 0:
            peer = partner
        return remote(
            ins[n_line + i],
            outs[n_line + i].at[seq],
            plane_send.at[i, d],
            plane_recv.at[i, seq],
            (peer, ep),
        )

    def fwd_copy(i, d):
        src = lax.rem(chip + d, chips) * 2 + core
        return remote(
            outs[n_line + i].at[src],
            outs[n_line + i].at[src],
            fwd_send.at[i, d],
            plane_recv.at[i, src],
            (partner, ep),
        )

    def plane_arrived(i, src):
        remote(
            ins[n_line + i],
            outs[n_line + i].at[src],
            plane_send.at[i, 0],
            plane_recv.at[i, src],
            (partner, ep),
        ).wait_recv()

    every = range(n_line)
    line_copies(0, every, lambda c: c.start())
    for i in range(n_plane):
        for d in range(chips):
            plane_copy(i, d).start()
    for i in range(total):
        pltpu.make_async_copy(ins[i], bufs[i], own_sem.at[i]).start()
    for i in range(total):
        pltpu.make_async_copy(ins[i], bufs[i], own_sem.at[i]).wait()
        mine = outs[i].at[ep if i < n_line else seq]
        pltpu.make_async_copy(bufs[i], mine, own_sem.at[i]).start()
    for step in range(1, n_ep - 1):
        line_arrived(step, every)
        line_copies(step, every, lambda c: c.start())
    for i in range(n_plane):
        for d in range(1, chips):
            plane_arrived(i, lax.rem(chip + d, chips) * 2 + core)
            fwd_copy(i, d).start()
    line_arrived(n_ep - 1, every)
    for i in range(n_plane):
        for d in range(chips):
            plane_arrived(i, lax.rem(chip + d, chips) * 2 + 1 - core)
    for i in range(total):
        mine = outs[i].at[ep if i < n_line else seq]
        pltpu.make_async_copy(bufs[i], mine, own_sem.at[i]).wait()
    for step in range(n_ep - 1):
        line_copies(step, every, lambda c: c.wait_send())
    for i in range(n_plane):
        for d in range(chips):
            plane_copy(i, d).wait_send()
        for d in range(1, chips):
            fwd_copy(i, d).wait_send()


def gathered(line, plane):
    n_seq, n_ep = lax.axis_size("seq"), lax.axis_size("ep")
    arrays = tuple(line) + tuple(plane)
    n_line, n_plane, chips = len(line), len(plane), n_seq // 2
    counts = [n_ep] * n_line + [n_seq] * n_plane
    anywhere = pl.BlockSpec(memory_space=pl.ANY)
    sem = pltpu.SemaphoreType.DMA
    return pl.pallas_call(
        functools.partial(gather_kernel, n_seq, n_ep, n_line, n_plane),
        out_shape=[jax.ShapeDtypeStruct((c,) + a.shape, a.dtype) for c, a in zip(counts, arrays)],
        in_specs=[anywhere] * len(arrays),
        out_specs=[anywhere] * len(arrays),
        scratch_shapes=[pltpu.VMEM(a.shape, a.dtype) for a in arrays]
        + [
            sem((len(arrays),)),
            sem((n_line, 2, n_ep)),
            sem((n_line, n_ep)),
            sem((n_plane, chips)),
            sem((n_plane, n_seq)),
            sem((n_plane, chips)),
        ],
        compiler_params=pltpu.CompilerParams(
            collective_id=0, has_side_effects=True, vmem_limit_bytes=16 << 20
        ),
        name="gather",
    )(*arrays)


def signal_all(barrier, n_seq, n_ep, seq, ep, line):
    for d in range(1, n_seq):
        pl.semaphore_signal(
            barrier, inc=1, device_id=(lax.rem(seq + d, n_seq), ep), device_id_type=MESH
        )
    count = jnp.int32(n_seq - 1)
    for d in line:
        there = (ep + d >= 0) & (ep + d < n_ep)

        @pl.when(there)
        def _():
            pl.semaphore_signal(barrier, inc=1, device_id=(seq, ep + d), device_id_type=MESH)

        count = count + there.astype(jnp.int32)
    pl.semaphore_wait(barrier, count)


def column_chunks(width, most=1024):
    return [(c, min(most, width - c)) for c in range(0, width, most)]


def moe_kernel(
    n_seq,
    n_ep,
    cap,
    x_ref,
    pick_ref,
    gate_ref,
    mixed_ref,
    win_hbm,
    wout_hbm,
    out_ref,
    held,
    staged,
    arrived,
    back,
    sums,
    mine,
    taken,
    joined,
    act,
    w_in,
    w_out,
    weight_sem,
    line_send,
    line_recv,
    send,
    recv,
    own,
    back_send,
    back_recv,
    back_own,
    sum_send,
    sum_recv,
):
    seq, ep = lax.axis_index("seq"), lax.axis_index("ep")
    rows, width = mixed_ref.shape
    slots = n_seq * cap
    hidden = wout_hbm.shape[0]
    in_copy = pltpu.make_async_copy(win_hbm, w_in, weight_sem.at[0])
    out_copy = pltpu.make_async_copy(wout_hbm, w_out, weight_sem.at[1])
    in_copy.start()
    out_copy.start()
    signal_all(pltpu.get_barrier_semaphore(), n_seq, n_ep, seq, ep, (-1, 1))

    def spread(buffer, c, size, value):
        for s in range(n_seq):
            buffer[s, :, pl.ds(c, size)] = value[s * cap : (s + 1) * cap].astype(jnp.bfloat16)

    def together(buffer, c, size, first, count):
        slabs = [buffer[first + s, :, c : c + size].astype(jnp.float32) for s in range(count)]
        return jnp.concatenate(slabs, axis=0).astype(jnp.bfloat16)

    def relay(step, src, away, act_on):
        @pl.when((src >= 0) & (src < n_ep) & (ep + away >= 0) & (ep + away < n_ep))
        def _():
            act_on(
                remote(
                    x_ref if step == 0 else held.at[src],
                    held.at[src],
                    line_send.at[(away + 1) // 2, step],
                    line_recv.at[src],
                    (seq, ep + away),
                )
            )

    def part(src, d):
        peer = lax.rem(seq + d, n_seq)
        return remote(
            staged.at[src, peer],
            arrived.at[src, seq],
            send.at[src, d],
            recv.at[src, seq],
            (peer, ep),
        )

    def own_part(src):
        return pltpu.make_async_copy(
            staged.at[src, seq], arrived.at[src, seq], own.at[src]
        )

    def back_part(src, d):
        peer = lax.rem(seq + d, n_seq)
        return remote(
            staged.at[src, peer],
            back.at[src, seq],
            back_send.at[src, d],
            back_recv.at[src, seq],
            (peer, ep),
        )

    def back_own_part(src):
        return pltpu.make_async_copy(
            staged.at[src, seq], back.at[src, seq], back_own.at[src]
        )

    def landing(at, step, way):
        return jnp.where(way == -1, n_ep, at) if step == 1 else at

    def sum_copy(at, step, way, i):
        c, size = column_chunks(width)[i]
        slot = landing(at, step, way)
        return remote(
            held.at[at, :, c : c + size],
            sums.at[slot, :, c : c + size],
            sum_send.at[at, i],
            sum_recv.at[slot, i],
            (seq, ep + way),
        )

    def sum_arrived(slot, i):
        c, size = column_chunks(width)[i]
        piece = sums.at[slot, :, c : c + size]
        remote(piece, piece, sum_send.at[0, 0], sum_recv.at[slot, i], (seq, ep)).wait_recv()

    def each(d, act_on):
        at = ep + d

        @pl.when((at >= 0) & (at < n_ep))
        def _():
            act_on(at)

    def hand_out(src, rows_ref):
        for c, size in column_chunks(width):
            picked = jnp.dot(
                pick_ref[src], rows_ref[:, c : c + size], preferred_element_type=jnp.float32
            )
            spread(staged.at[src], c, size, picked)
        for d in range(1, n_seq):
            part(src, d).start()
        own_part(src).start()

    def expert(src):
        own_part(src).wait()
        for d in range(1, n_seq):
            peer = lax.rem(seq + d, n_seq)
            remote(
                staged.at[src, seq],
                arrived.at[src, peer],
                send.at[src, 0],
                recv.at[src, peer],
                (peer, ep),
            ).wait_recv()

        group = n_seq if slots % 16 else 2
        for s in range(0, n_seq, group):
            taken[s * cap : (s + group) * cap, :] = together(arrived.at[src], 0, width, s, group)

        def up_columns(c, size):
            joined[:, pl.ds(c, size)] = jnp.dot(
                taken[...], w_in[:, pl.ds(c, size)], preferred_element_type=jnp.float32
            )

        @pl.loop(0, width // 512)
        def _(i):
            up_columns(pl.multiple_of(i * 512, 512), 512)

        if width % 512:
            up_columns(width // 512 * 512, width % 512)

        @pl.loop(0, slots // 16)
        def _(i):
            r = pl.ds(pl.multiple_of(i * 16, 16), 16)
            gate = joined[r, 0:hidden]
            up = joined[r, hidden : 2 * hidden]
            act[r, :] = ((up + 1.0) * gate * jax.nn.sigmoid(1.702 * gate)).astype(jnp.bfloat16)

        for d in range(1, n_seq):
            part(src, d).wait_send()

        def down_columns(c, size):
            value = jnp.dot(
                act[...], w_out[:, pl.ds(c, size)], preferred_element_type=jnp.float32
            )
            spread(staged.at[src], c, size, value)

        @pl.loop(0, width // 512)
        def _(i):
            down_columns(pl.multiple_of(i * 512, 512), 512)

        if width % 512:
            down_columns(width // 512 * 512, width % 512)
        for d in range(1, n_seq):
            back_part(src, d).start()
        back_own_part(src).start()

    def gather_up(at, finish):
        back_own_part(at).wait()
        for d in range(1, n_seq):
            peer = lax.rem(seq + d, n_seq)
            remote(
                staged.at[at, seq],
                back.at[at, peer],
                back_send.at[at, 0],
                back_recv.at[at, peer],
                (peer, ep),
            ).wait_recv()
        for i, (c, size) in enumerate(column_chunks(width)):
            results = together(back.at[at], c, size, 0, n_seq)
            three = jnp.dot(gate_ref[at], results, preferred_element_type=jnp.float32)
            finish(i, c, size, three[:rows] + three[rows : 2 * rows] + three[2 * rows :])

    def pass_on(step, way):
        at = ep + way * step

        @pl.when((at >= 0) & (at < n_ep))
        def _():
            relay(step, at, -way, lambda c: c.wait_send())

            def finish(i, c, size, value):
                before = ep - way
                joins = (before >= 0) & (before < n_ep)

                @pl.when(joins)
                def _():
                    sum_arrived(at, i)
                    sofar = sums[at, :, c : c + size].astype(jnp.float32)
                    held[at, :, c : c + size] = (value + sofar).astype(jnp.bfloat16)

                @pl.when(jnp.logical_not(joins))
                def _():
                    held[at, :, c : c + size] = value.astype(jnp.bfloat16)

                sum_copy(at, step, way, i).start()

            gather_up(at, finish)

    relay(0, ep, 1, lambda c: c.start())
    relay(0, ep, -1, lambda c: c.start())
    hand_out(ep, x_ref)
    for step in range(1, n_ep):
        for way in (1, -1):
            src = ep - way * step

            @pl.when((src >= 0) & (src < n_ep))
            def _():
                remote(
                    x_ref, held.at[src], line_send.at[0, 0], line_recv.at[src], (seq, ep)
                ).wait_recv()

            relay(step, src, way, lambda c: c.start())
        for way in (1, -1):
            each(-way * step, lambda at: hand_out(at, held.at[at]))
        if step == 1:
            in_copy.wait()
            out_copy.wait()
            expert(ep)
        else:
            for way in (1, -1):
                each(-way * (step - 1), expert)
    toward = jnp.where(2 * ep < n_ep, 1, -1)
    at_end = (ep == 0) | (ep == n_ep - 1)

    @pl.when(at_end)
    def _():
        for step in range(1, n_ep - 2):
            pass_on(step, toward)

    for way in (1, -1):
        each(-way * (n_ep - 1), expert)

    @pl.when(jnp.logical_not(at_end))
    def _():
        for step in range(1, n_ep - 2):
            pass_on(step, toward)

    for step in range(max(1, n_ep - 2), n_ep):
        pass_on(step, toward)

    def keep(i, c, size, value):
        mine[:, c : c + size] = mixed_ref[:, c : c + size] + value

    gather_up(ep, keep)

    for step in range(1, n_ep // 2):
        pass_on(step, -toward)

    def add(slot):
        for i, (c, size) in enumerate(column_chunks(width)):
            sum_arrived(slot, i)
            mine[:, c : c + size] += sums[slot, :, c : c + size].astype(jnp.float32)

    @pl.when(ep > 0)
    def _():
        add(ep)

    @pl.when(ep < n_ep - 1)
    def _():
        add(n_ep)

    for c, size in column_chunks(width):
        out_ref[:, c : c + size] = mine[:, c : c + size].astype(jnp.bfloat16)
    for step in range(1, n_ep):
        for way in (1, -1):

            def sent(at):
                for i in range(len(column_chunks(width))):
                    sum_copy(at, step, way, i).wait_send()

            each(way * step, sent)
    for way in (1, -1):
        relay(0, ep, way, lambda c: c.wait_send())
    for src in range(n_ep):
        for d in range(1, n_seq):
            back_part(src, d).wait_send()


def mixture(rows_in, picks, gates, mixed, w_in, w_out, cap):
    n_seq, n_ep = lax.axis_size("seq"), lax.axis_size("ep")
    rows, width = mixed.shape
    hidden = w_out.shape[0]
    slots = n_seq * cap
    sem = pltpu.SemaphoreType.DMA
    vmem = pl.BlockSpec(memory_space=pltpu.VMEM)
    anywhere = pl.BlockSpec(memory_space=pl.ANY)
    return pl.pallas_call(
        functools.partial(moe_kernel, n_seq, n_ep, cap),
        out_shape=jax.ShapeDtypeStruct((rows, width), jnp.bfloat16),
        in_specs=[vmem, vmem, vmem, vmem, anywhere, anywhere],
        out_specs=vmem,
        scratch_shapes=[
            pltpu.VMEM((n_ep, rows, width), jnp.bfloat16),
            pltpu.VMEM((n_ep, n_seq, cap, width), jnp.bfloat16),
            pltpu.VMEM((n_ep, n_seq, cap, width), jnp.bfloat16),
            pltpu.VMEM((n_ep, n_seq, cap, width), jnp.bfloat16),
            pltpu.VMEM((n_ep + 1, rows, width), jnp.bfloat16),
            pltpu.VMEM((rows, width), jnp.float32),
            pltpu.VMEM((slots, width), jnp.bfloat16),
            pltpu.VMEM((slots, width), jnp.float32),
            pltpu.VMEM((slots, hidden), jnp.bfloat16),
            pltpu.VMEM(w_in.shape, jnp.bfloat16),
            pltpu.VMEM(w_out.shape, jnp.bfloat16),
            sem((2,)),
            sem((2, n_ep)),
            sem((n_ep,)),
            sem((n_ep, n_seq)),
            sem((n_ep, n_seq)),
            sem((n_ep,)),
            sem((n_ep, n_seq)),
            sem((n_ep, n_seq)),
            sem((n_ep,)),
            sem((n_ep, len(column_chunks(width)))),
            sem((n_ep + 1, len(column_chunks(width)))),
        ],
        compiler_params=pltpu.CompilerParams(
            collective_id=1, has_side_effects=True, vmem_limit_bytes=64000 << 10
        ),
        name="mixture",
    )(rows_in, picks, gates, mixed, w_in, w_out)


def slot_of(ids, capacity):
    count = ids.size
    flat = ids.reshape(-1)
    earlier = jnp.arange(count)[:, None] > jnp.arange(count)[None, :]
    same = (flat[:, None] == flat[None, :]) & earlier
    ranks = jnp.sum(same.astype(jnp.int32), axis=1)
    return (flat * capacity + ranks).reshape(ids.shape)


def three_parts(x):
    high = lax.reduce_precision(x, 8, 7)
    rest = x - high
    middle = lax.reduce_precision(rest, 8, 7)
    return high.astype(jnp.bfloat16), middle.astype(jnp.bfloat16), (rest - middle).astype(jnp.bfloat16)


def by_rows(x):
    return with_layout_constraint(x, Layout(tuple(range(x.ndim))))


def body(
    activations,
    attn_gain,
    query_weight,
    key_weight,
    value_weight,
    output_weight,
    sink_logits,
    mlp_gain,
    expert_ids,
    expert_gates,
    expert_in,
    expert_out,
):
    own_rows = activations.shape[0]
    width_dim = activations.shape[1]
    seq_count = lax.axis_size("seq")
    ep_count = lax.axis_size("ep")
    tok_rows = own_rows * ep_count
    act_f32 = activations.astype(jnp.float32)
    normed_own = normed(act_f32, attn_gain).astype(jnp.bfloat16)
    q_cols = query_weight.shape[1]
    kv_cols = key_weight.shape[1]
    experts_all = seq_count * ep_count
    top_k = expert_ids.shape[1]
    capacity = max(2, 3 * own_rows * top_k // (2 * experts_all))
    capacity = -(-capacity // 8) * 8
    (normed_all, line_slots, line_gates, *shard_rows) = gathered(
        (normed_own, slot_of(expert_ids, capacity).T, expert_gates.T),
        (query_weight, key_weight, value_weight),
    )
    normed_all, out_cols = lax.optimization_barrier((normed_all, output_weight.T))
    out_rows = lax.all_gather(out_cols, "seq", axis=0, tiled=True)
    normed_all = normed_all.reshape(tok_rows, width_dim)
    shard_rows = [rows.reshape(width_dim, -1) for rows in shard_rows]
    q_lin, k_lin, v_lin = tuple(
        (
            jnp.dot(normed_all, weight_rows, preferred_element_type=jnp.float32)
            for weight_rows in shard_rows
        )
    )
    q_lin, k_lin = by_rows(q_lin), by_rows(k_lin)
    first_pos = lax.axis_index("seq") * tok_rows
    positions = (first_pos + jnp.arange(tok_rows, dtype=jnp.int32)).astype(jnp.float32)
    q_heads = q_cols // HD
    kv_heads = kv_cols // HD
    group_size = q_heads // kv_heads
    queries = (
        rotate(q_lin.reshape(tok_rows, q_heads, HD), positions)
        .astype(jnp.bfloat16)
        .reshape(tok_rows, kv_heads, group_size, HD)
    )
    keys_rot = (
        rotate(k_lin.reshape(tok_rows, kv_heads, HD), positions)
        .astype(jnp.bfloat16)
        .reshape(tok_rows, kv_cols)
    )
    values_cast = v_lin.astype(jnp.bfloat16)
    prev_keys, prev_values = passed_along(
        (keys_rot[tok_rows - WIN :], values_cast[tok_rows - WIN :]), "seq", 1
    )
    key_all = jnp.concatenate([prev_keys, keys_rot], axis=0).reshape(WIN + tok_rows, kv_heads, HD)
    val_all = jnp.concatenate([prev_values, values_cast], axis=0).reshape(
        WIN + tok_rows, kv_heads, HD
    )
    block_len = min(tok_rows, 512)
    sink_grid = sink_logits.reshape(kv_heads, group_size)

    def one_block(block):
        row_first = block * block_len
        return attend(queries, key_all, val_all, sink_grid, first_pos + row_first, WIN)

    attended = lax.map(one_block, jnp.arange(tok_rows // block_len, dtype=jnp.int32)).reshape(
        tok_rows, q_cols
    )
    head_partial = lax.dot_general(
        attended, out_rows, (((1,), (1,)), ((), ())), preferred_element_type=jnp.float32
    ).astype(jnp.bfloat16)
    head_sum = lax.psum_scatter(
        by_rows(head_partial), "ep", scatter_dimension=0, tiled=True
    ).astype(jnp.float32)
    mixed = act_f32 + head_sum
    mlp_in = normed(mixed, mlp_gain).astype(jnp.bfloat16)
    plane_rows = seq_count * capacity
    place = jnp.arange(plane_rows, dtype=jnp.int32)
    first_slots = (place // capacity * ep_count + lax.axis_index("ep")) * capacity
    plane_slots = first_slots + place % capacity
    picks = sum(
        (line_slots[:, k, None, :] == plane_slots[None, :, None]).astype(jnp.bfloat16)
        for k in range(top_k)
    )
    gate_at = sum(
        jnp.where(
            line_slots[:, k, :, None] == plane_slots[None, None, :],
            line_gates[:, k, :, None],
            0.0,
        )
        for k in range(top_k)
    )
    gate_parts = jnp.concatenate(three_parts(gate_at), axis=1)
    return mixture(
        mlp_in, picks, gate_parts, mixed, expert_in[0], expert_out[0], capacity
    )


def solution(mesh):
    return jax.shard_map(
        body,
        mesh=mesh,
        in_specs=(
            P(("seq", "ep"), None),
            P(),
            P("seq", "ep"),
            P("seq", "ep"),
            P("seq", "ep"),
            P("ep", "seq"),
            P("ep"),
            P(),
            P(("seq", "ep"), None),
            P(("seq", "ep"), None),
            P(("seq", "ep"), None, None),
            P(("seq", "ep"), None, None),
        ),
        out_specs=P(("seq", "ep"), None),
        check_vma=False,
    )
```

```python
import functools

import jax
import jax.numpy as jnp
from jax import lax
from jax.experimental import pallas as pl
from jax.experimental.layout import Layout, with_layout_constraint
from jax.experimental.pallas import tpu as pltpu
from jax.sharding import PartitionSpec as P

MESH = pl.DeviceIdType.MESH

HD = 64
WIN = 128


def passed_along(x, axis, by):
    count = lax.axis_size(axis)
    pairs = [(i, i + by) for i in range(count) if 0 <= i + by < count]
    return lax.ppermute(x, axis, pairs)


def normed(rows_f32, gain_vec):
    inv_rms = lax.rsqrt(jnp.mean(rows_f32 * rows_f32, axis=-1, keepdims=True) + 1e-05)
    return rows_f32 * inv_rms * gain_vec


def rotate(head_vals, positions):
    half_dim = head_vals.shape[-1] // 2
    inv_freq = 150000.0 ** (-jnp.arange(half_dim, dtype=jnp.float32) / half_dim)
    angles = positions[:, None] * inv_freq[None, :]
    cosines = jnp.cos(angles)[:, None, :]
    sines = jnp.sin(angles)[:, None, :]
    first = head_vals[..., :half_dim]
    second = head_vals[..., half_dim:]
    return jnp.concatenate(
        [first * cosines - second * sines, second * cosines + first * sines], axis=-1
    )


def attend(queries, key_rows, val_rows, sink_grid, query_first, win_len):
    scores = (
        jnp.einsum("qkgd,jkd->kgqj", queries, key_rows, preferred_element_type=jnp.float32) * 0.125
    )
    q_pos = query_first + jnp.arange(queries.shape[0], dtype=jnp.int32)
    k_pos = query_first - win_len + jnp.arange(key_rows.shape[0], dtype=jnp.int32)
    offset = q_pos[:, None] - k_pos[None, :]
    allowed = (offset >= 0) & (offset < win_len) & (k_pos[None, :] >= 0)
    scores = jnp.where(allowed, scores, jnp.float32(-1e30))
    peak_val = jnp.maximum(jnp.max(scores, axis=-1), sink_grid[:, :, None])
    exp_terms = jnp.exp(scores - peak_val[..., None])
    denominator = jnp.sum(exp_terms, axis=-1) + jnp.exp(sink_grid[:, :, None] - peak_val)
    weights = (exp_terms / denominator[..., None]).astype(jnp.bfloat16)
    mixed_vals = jnp.einsum("kgqj,jkd->qkgd", weights, val_rows, preferred_element_type=jnp.float32)
    return mixed_vals.astype(jnp.bfloat16)


def remote(src, dst, send_sem, recv_sem, device):
    return pltpu.make_async_remote_copy(
        src_ref=src,
        dst_ref=dst,
        send_sem=send_sem,
        recv_sem=recv_sem,
        device_id=device,
        device_id_type=MESH,
    )


def gather_kernel(n_seq, n_ep, n_line, n_plane, *refs):
    total = n_line + n_plane
    ins, outs, bufs = refs[:total], refs[total : 2 * total], refs[2 * total : 3 * total]
    own_sem, line_send, line_recv, plane_send, plane_recv, fwd_send, turn_send, turn_recv = refs[
        3 * total :
    ]
    seq, ep = lax.axis_index("seq"), lax.axis_index("ep")
    chips = n_seq // 2
    chip, core = seq // 2, seq % 2
    partner = chip * 2 + 1 - core

    barrier = pltpu.get_barrier_semaphore()

    @pl.when(ep > 0)
    def _():
        pl.semaphore_signal(barrier, inc=1, device_id=(seq, ep - 1), device_id_type=MESH)

    @pl.when(ep < n_ep - 1)
    def _():
        pl.semaphore_signal(barrier, inc=1, device_id=(seq, ep + 1), device_id_type=MESH)

    for d in range(1, chips):
        peer = lax.rem(chip + d, chips) * 2 + core
        pl.semaphore_signal(barrier, inc=1, device_id=(peer, ep), device_id_type=MESH)
    pl.semaphore_signal(barrier, inc=1, device_id=(partner, ep), device_id_type=MESH)
    neighbours = (ep > 0).astype(jnp.int32) + (ep < n_ep - 1).astype(jnp.int32)
    pl.semaphore_wait(barrier, chips + neighbours)

    def line_copies(step, which, act):
        for i in which:
            left_src, right_src = ep - step, ep + step

            @pl.when((left_src >= 0) & (ep < n_ep - 1))
            def _():
                src = ins[i] if step == 0 else outs[i].at[left_src]
                act(
                    remote(
                        src,
                        outs[i].at[left_src],
                        line_send.at[i, 0, step],
                        line_recv.at[i, left_src],
                        (seq, ep + 1),
                    )
                )

            @pl.when((right_src < n_ep) & (ep > 0))
            def _():
                src = ins[i] if step == 0 else outs[i].at[right_src]
                act(
                    remote(
                        src,
                        outs[i].at[right_src],
                        line_send.at[i, 1, step],
                        line_recv.at[i, right_src],
                        (seq, ep - 1),
                    )
                )

    def line_arrived(step, which):
        for i in which:
            for src in (ep - step, ep + step):

                @pl.when((src >= 0) & (src < n_ep))
                def _():
                    remote(
                        ins[i],
                        outs[i].at[src],
                        line_send.at[i, 0, 0],
                        line_recv.at[i, src],
                        (seq, ep),
                    ).wait_recv()

    square = chips == 4
    half = ins[n_line].shape[0] // 32 * 16
    if square:
        beside, above = chip + 1 - 2 * (chip % 2), lax.rem(chip + 2, 4)
        across = 3 - chip
        targets = {0: partner, 1: beside * 2 + core, 2: above * 2 + core}
    else:
        targets = {d: lax.rem(chip + d, chips) * 2 + core for d in range(1, chips)}
        targets[0] = partner
    peers = [d for d in targets if d != 0]

    def plane_copy(i, d):
        return remote(
            ins[n_line + i],
            outs[n_line + i].at[seq],
            plane_send.at[i, d],
            plane_recv.at[i, seq],
            (targets[d], ep),
        )

    def fwd_copy(i, d, src):
        whole = outs[n_line + i].at[src]
        return remote(whole, whole, fwd_send.at[i, d], plane_recv.at[i, src], (partner, ep))

    def turn_copy(i, d):
        src = targets[d]
        rows = ins[n_line + i].shape[0]
        part = pl.ds(0, half) if d == 1 else pl.ds(half, rows - half)
        piece = outs[n_line + i].at[src, part]
        arrival = plane_recv if d == 1 else turn_recv
        return remote(
            piece, piece, turn_send.at[i, d], arrival.at[i, src], (targets[3 - d], ep)
        )

    def plane_arrived(i, src):
        whole = outs[n_line + i].at[src]
        remote(whole, whole, plane_send.at[i, 0], plane_recv.at[i, src], (partner, ep)).wait_recv()

    def halves_arrived(i, src):
        rows = ins[n_line + i].shape[0]
        for part, arrival in ((pl.ds(0, half), plane_recv), (pl.ds(half, rows - half), turn_recv)):
            piece = outs[n_line + i].at[src, part]
            remote(piece, piece, plane_send.at[i, 0], arrival.at[i, src], (partner, ep)).wait_recv()

    def near_arrived(which):
        for i in which:
            for d in peers:
                plane_arrived(i, targets[d])
                if square:
                    turn_copy(i, d).start()
                fwd_copy(i, d, targets[d]).start()

    def across_arrived(which):
        if square:
            for i in which:
                halves_arrived(i, across * 2 + core)
                fwd_copy(i, 3, across * 2 + core).start()

    every = range(n_line)
    last = n_plane - 1
    line_copies(0, every, lambda c: c.start())
    for i in range(n_plane):
        for d in (*peers, 0):
            plane_copy(i, d).start()
    for i in range(total):
        pltpu.make_async_copy(ins[i], bufs[i], own_sem.at[i]).start()
    for i in range(total):
        pltpu.make_async_copy(ins[i], bufs[i], own_sem.at[i]).wait()
        mine = outs[i].at[ep if i < n_line else seq]
        pltpu.make_async_copy(bufs[i], mine, own_sem.at[i]).start()
    for step in range(1, n_ep - 1):
        line_arrived(step, every)
        line_copies(step, every, lambda c: c.start())
        if step == 1:
            near_arrived(range(last))
    near_arrived([last])
    across_arrived(range(n_plane))
    line_arrived(n_ep - 1, every)
    for i in range(n_plane):
        for other in range(chips):
            plane_arrived(i, other * 2 + 1 - core)
    for i in range(total):
        mine = outs[i].at[ep if i < n_line else seq]
        pltpu.make_async_copy(bufs[i], mine, own_sem.at[i]).wait()
    for step in range(n_ep - 1):
        line_copies(step, every, lambda c: c.wait_send())
    for i in range(n_plane):
        for d in (*peers, 0):
            plane_copy(i, d).wait_send()
        for d in peers:
            fwd_copy(i, d, targets[d]).wait_send()
            if square:
                turn_copy(i, d).wait_send()
        if square:
            fwd_copy(i, 3, across * 2 + core).wait_send()


def gathered(line, plane):
    n_seq, n_ep = lax.axis_size("seq"), lax.axis_size("ep")
    arrays = tuple(line) + tuple(plane)
    n_line, n_plane, chips = len(line), len(plane), n_seq // 2
    counts = [n_ep] * n_line + [n_seq] * n_plane
    anywhere = pl.BlockSpec(memory_space=pl.ANY)
    sem = pltpu.SemaphoreType.DMA
    return pl.pallas_call(
        functools.partial(gather_kernel, n_seq, n_ep, n_line, n_plane),
        out_shape=[jax.ShapeDtypeStruct((c,) + a.shape, a.dtype) for c, a in zip(counts, arrays)],
        in_specs=[anywhere] * len(arrays),
        out_specs=[anywhere] * len(arrays),
        scratch_shapes=[pltpu.VMEM(a.shape, a.dtype) for a in arrays]
        + [
            sem((len(arrays),)),
            sem((n_line, 2, n_ep)),
            sem((n_line, n_ep)),
            sem((n_plane, chips)),
            sem((n_plane, n_seq)),
            sem((n_plane, chips)),
            sem((n_plane, 3)),
            sem((n_plane, n_seq)),
        ],
        compiler_params=pltpu.CompilerParams(
            collective_id=0, has_side_effects=True, vmem_limit_bytes=16 << 20
        ),
        name="gather",
    )(*arrays)


def signal_all(barrier, n_seq, n_ep, seq, ep, line):
    for d in range(1, n_seq):
        pl.semaphore_signal(
            barrier, inc=1, device_id=(lax.rem(seq + d, n_seq), ep), device_id_type=MESH
        )
    count = jnp.int32(n_seq - 1)
    for d in line:
        there = (ep + d >= 0) & (ep + d < n_ep)

        @pl.when(there)
        def _():
            pl.semaphore_signal(barrier, inc=1, device_id=(seq, ep + d), device_id_type=MESH)

        count = count + there.astype(jnp.int32)
    pl.semaphore_wait(barrier, count)


def column_chunks(width, most=1024):
    return [(c, min(most, width - c)) for c in range(0, width, most)]


def moe_kernel(
    n_seq,
    n_ep,
    cap,
    x_ref,
    pick_ref,
    gate_ref,
    mixed_ref,
    win_hbm,
    wout_hbm,
    out_ref,
    held,
    staged,
    arrived,
    back,
    sums,
    mine,
    taken,
    joined,
    act,
    w_in,
    w_out,
    weight_sem,
    line_send,
    line_recv,
    send,
    recv,
    own,
    back_send,
    back_recv,
    back_own,
    sum_send,
    sum_recv,
):
    seq, ep = lax.axis_index("seq"), lax.axis_index("ep")
    rows, width = mixed_ref.shape
    slots = n_seq * cap
    hidden = wout_hbm.shape[0]
    in_copy = pltpu.make_async_copy(win_hbm, w_in, weight_sem.at[0])
    out_copy = pltpu.make_async_copy(wout_hbm, w_out, weight_sem.at[1])
    in_copy.start()
    out_copy.start()
    signal_all(pltpu.get_barrier_semaphore(), n_seq, n_ep, seq, ep, (-1, 1))

    def spread(buffer, c, size, value):
        for s in range(n_seq):
            buffer[s, :, pl.ds(c, size)] = value[s * cap : (s + 1) * cap].astype(jnp.bfloat16)

    def together(buffer, c, size, first, count):
        slabs = [buffer[first + s, :, c : c + size].astype(jnp.float32) for s in range(count)]
        return jnp.concatenate(slabs, axis=0).astype(jnp.bfloat16)

    def relay(step, src, away, act_on):
        @pl.when((src >= 0) & (src < n_ep) & (ep + away >= 0) & (ep + away < n_ep))
        def _():
            act_on(
                remote(
                    x_ref if step == 0 else held.at[src],
                    held.at[src],
                    line_send.at[(away + 1) // 2, step],
                    line_recv.at[src],
                    (seq, ep + away),
                )
            )

    def part(src, d):
        peer = lax.rem(seq + d, n_seq)
        return remote(
            staged.at[src, peer],
            arrived.at[src, seq],
            send.at[src, d],
            recv.at[src, seq],
            (peer, ep),
        )

    def own_part(src):
        return pltpu.make_async_copy(
            staged.at[src, seq], arrived.at[src, seq], own.at[src]
        )

    def back_part(src, d):
        peer = lax.rem(seq + d, n_seq)
        return remote(
            staged.at[src, peer],
            back.at[src, seq],
            back_send.at[src, d],
            back_recv.at[src, seq],
            (peer, ep),
        )

    def back_own_part(src):
        return pltpu.make_async_copy(
            staged.at[src, seq], back.at[src, seq], back_own.at[src]
        )

    def landing(at, step, way):
        return jnp.where(way == -1, n_ep, at) if step == 1 else at

    def sum_copy(at, step, way, i):
        c, size = column_chunks(width)[i]
        slot = landing(at, step, way)
        return remote(
            held.at[at, :, c : c + size],
            sums.at[slot, :, c : c + size],
            sum_send.at[at, i],
            sum_recv.at[slot, i],
            (seq, ep + way),
        )

    def sum_arrived(slot, i):
        c, size = column_chunks(width)[i]
        piece = sums.at[slot, :, c : c + size]
        remote(piece, piece, sum_send.at[0, 0], sum_recv.at[slot, i], (seq, ep)).wait_recv()

    def each(d, act_on):
        at = ep + d

        @pl.when((at >= 0) & (at < n_ep))
        def _():
            act_on(at)

    def hand_out(src, rows_ref):
        for c, size in column_chunks(width):
            picked = jnp.dot(
                pick_ref[src], rows_ref[:, c : c + size], preferred_element_type=jnp.float32
            )
            spread(staged.at[src], c, size, picked)
        for d in range(1, n_seq):
            part(src, d).start()
        own_part(src).start()

    def expert(src):
        own_part(src).wait()
        for d in range(1, n_seq):
            peer = lax.rem(seq + d, n_seq)
            remote(
                staged.at[src, seq],
                arrived.at[src, peer],
                send.at[src, 0],
                recv.at[src, peer],
                (peer, ep),
            ).wait_recv()

        group = n_seq if slots % 16 else 2
        for s in range(0, n_seq, group):
            taken[s * cap : (s + group) * cap, :] = together(arrived.at[src], 0, width, s, group)

        def up_columns(c, size):
            joined[:, pl.ds(c, size)] = jnp.dot(
                taken[...], w_in[:, pl.ds(c, size)], preferred_element_type=jnp.float32
            )

        @pl.loop(0, width // 512)
        def _(i):
            up_columns(pl.multiple_of(i * 512, 512), 512)

        if width % 512:
            up_columns(width // 512 * 512, width % 512)

        @pl.loop(0, slots // 16)
        def _(i):
            r = pl.ds(pl.multiple_of(i * 16, 16), 16)
            gate = joined[r, 0:hidden]
            up = joined[r, hidden : 2 * hidden]
            act[r, :] = ((up + 1.0) * gate * jax.nn.sigmoid(1.702 * gate)).astype(jnp.bfloat16)

        for d in range(1, n_seq):
            part(src, d).wait_send()

        def down_columns(c, size):
            value = jnp.dot(
                act[...], w_out[:, pl.ds(c, size)], preferred_element_type=jnp.float32
            )
            spread(staged.at[src], c, size, value)

        @pl.loop(0, width // 512)
        def _(i):
            down_columns(pl.multiple_of(i * 512, 512), 512)

        if width % 512:
            down_columns(width // 512 * 512, width % 512)
        for d in range(1, n_seq):
            back_part(src, d).start()
        back_own_part(src).start()

    def gather_up(at, finish):
        back_own_part(at).wait()
        for d in range(1, n_seq):
            peer = lax.rem(seq + d, n_seq)
            remote(
                staged.at[at, seq],
                back.at[at, peer],
                back_send.at[at, 0],
                back_recv.at[at, peer],
                (peer, ep),
            ).wait_recv()
        for i, (c, size) in enumerate(column_chunks(width)):
            results = together(back.at[at], c, size, 0, n_seq)
            three = jnp.dot(gate_ref[at], results, preferred_element_type=jnp.float32)
            finish(i, c, size, three[:rows] + three[rows : 2 * rows] + three[2 * rows :])

    def pass_on(step, way):
        at = ep + way * step

        @pl.when((at >= 0) & (at < n_ep))
        def _():
            relay(step, at, -way, lambda c: c.wait_send())

            def finish(i, c, size, value):
                before = ep - way
                joins = (before >= 0) & (before < n_ep)

                @pl.when(joins)
                def _():
                    sum_arrived(at, i)
                    sofar = sums[at, :, c : c + size].astype(jnp.float32)
                    held[at, :, c : c + size] = (value + sofar).astype(jnp.bfloat16)

                @pl.when(jnp.logical_not(joins))
                def _():
                    held[at, :, c : c + size] = value.astype(jnp.bfloat16)

                sum_copy(at, step, way, i).start()

            gather_up(at, finish)

    relay(0, ep, 1, lambda c: c.start())
    relay(0, ep, -1, lambda c: c.start())
    hand_out(ep, x_ref)
    for step in range(1, n_ep):
        for way in (1, -1):
            src = ep - way * step

            @pl.when((src >= 0) & (src < n_ep))
            def _():
                remote(
                    x_ref, held.at[src], line_send.at[0, 0], line_recv.at[src], (seq, ep)
                ).wait_recv()

            relay(step, src, way, lambda c: c.start())
        for way in (1, -1):
            each(-way * step, lambda at: hand_out(at, held.at[at]))
        if step == 1:
            in_copy.wait()
            out_copy.wait()
            expert(ep)
        else:
            for way in (1, -1):
                each(-way * (step - 1), expert)
    toward = jnp.where(2 * ep < n_ep, 1, -1)
    at_end = (ep == 0) | (ep == n_ep - 1)

    @pl.when(at_end)
    def _():
        for step in range(1, n_ep - 2):
            pass_on(step, toward)

    for way in (1, -1):
        each(-way * (n_ep - 1), expert)

    @pl.when(jnp.logical_not(at_end))
    def _():
        for step in range(1, n_ep - 2):
            pass_on(step, toward)

    for step in range(max(1, n_ep - 2), n_ep):
        pass_on(step, toward)

    def keep(i, c, size, value):
        mine[:, c : c + size] = mixed_ref[:, c : c + size] + value

    gather_up(ep, keep)

    for step in range(1, n_ep // 2):
        pass_on(step, -toward)

    def add(slot):
        for i, (c, size) in enumerate(column_chunks(width)):
            sum_arrived(slot, i)
            mine[:, c : c + size] += sums[slot, :, c : c + size].astype(jnp.float32)

    @pl.when(ep > 0)
    def _():
        add(ep)

    @pl.when(ep < n_ep - 1)
    def _():
        add(n_ep)

    for c, size in column_chunks(width):
        out_ref[:, c : c + size] = mine[:, c : c + size].astype(jnp.bfloat16)
    for step in range(1, n_ep):
        for way in (1, -1):

            def sent(at):
                for i in range(len(column_chunks(width))):
                    sum_copy(at, step, way, i).wait_send()

            each(way * step, sent)
    for way in (1, -1):
        relay(0, ep, way, lambda c: c.wait_send())
    for src in range(n_ep):
        for d in range(1, n_seq):
            back_part(src, d).wait_send()


def mixture(rows_in, picks, gates, mixed, w_in, w_out, cap):
    n_seq, n_ep = lax.axis_size("seq"), lax.axis_size("ep")
    rows, width = mixed.shape
    hidden = w_out.shape[0]
    slots = n_seq * cap
    sem = pltpu.SemaphoreType.DMA
    vmem = pl.BlockSpec(memory_space=pltpu.VMEM)
    anywhere = pl.BlockSpec(memory_space=pl.ANY)
    return pl.pallas_call(
        functools.partial(moe_kernel, n_seq, n_ep, cap),
        out_shape=jax.ShapeDtypeStruct((rows, width), jnp.bfloat16),
        in_specs=[vmem, vmem, vmem, vmem, anywhere, anywhere],
        out_specs=vmem,
        scratch_shapes=[
            pltpu.VMEM((n_ep, rows, width), jnp.bfloat16),
            pltpu.VMEM((n_ep, n_seq, cap, width), jnp.bfloat16),
            pltpu.VMEM((n_ep, n_seq, cap, width), jnp.bfloat16),
            pltpu.VMEM((n_ep, n_seq, cap, width), jnp.bfloat16),
            pltpu.VMEM((n_ep + 1, rows, width), jnp.bfloat16),
            pltpu.VMEM((rows, width), jnp.float32),
            pltpu.VMEM((slots, width), jnp.bfloat16),
            pltpu.VMEM((slots, width), jnp.float32),
            pltpu.VMEM((slots, hidden), jnp.bfloat16),
            pltpu.VMEM(w_in.shape, jnp.bfloat16),
            pltpu.VMEM(w_out.shape, jnp.bfloat16),
            sem((2,)),
            sem((2, n_ep)),
            sem((n_ep,)),
            sem((n_ep, n_seq)),
            sem((n_ep, n_seq)),
            sem((n_ep,)),
            sem((n_ep, n_seq)),
            sem((n_ep, n_seq)),
            sem((n_ep,)),
            sem((n_ep, len(column_chunks(width)))),
            sem((n_ep + 1, len(column_chunks(width)))),
        ],
        compiler_params=pltpu.CompilerParams(
            collective_id=1, has_side_effects=True, vmem_limit_bytes=64000 << 10
        ),
        name="mixture",
    )(rows_in, picks, gates, mixed, w_in, w_out)


def slot_of(ids, capacity):
    count = ids.size
    flat = ids.reshape(-1)
    earlier = jnp.arange(count)[:, None] > jnp.arange(count)[None, :]
    same = (flat[:, None] == flat[None, :]) & earlier
    ranks = jnp.sum(same.astype(jnp.int32), axis=1)
    return (flat * capacity + ranks).reshape(ids.shape)


def three_parts(x):
    high = lax.reduce_precision(x, 8, 7)
    rest = x - high
    middle = lax.reduce_precision(rest, 8, 7)
    return high.astype(jnp.bfloat16), middle.astype(jnp.bfloat16), (rest - middle).astype(jnp.bfloat16)


def by_rows(x):
    return with_layout_constraint(x, Layout(tuple(range(x.ndim))))


def body(
    activations,
    attn_gain,
    query_weight,
    key_weight,
    value_weight,
    output_weight,
    sink_logits,
    mlp_gain,
    expert_ids,
    expert_gates,
    expert_in,
    expert_out,
):
    own_rows = activations.shape[0]
    width_dim = activations.shape[1]
    seq_count = lax.axis_size("seq")
    ep_count = lax.axis_size("ep")
    tok_rows = own_rows * ep_count
    act_f32 = activations.astype(jnp.float32)
    normed_own = normed(act_f32, attn_gain).astype(jnp.bfloat16)
    q_cols = query_weight.shape[1]
    kv_cols = key_weight.shape[1]
    experts_all = seq_count * ep_count
    top_k = expert_ids.shape[1]
    capacity = max(2, 3 * own_rows * top_k // (2 * experts_all))
    capacity = -(-capacity // 8) * 8
    (normed_all, line_slots, line_gates, *shard_rows) = gathered(
        (normed_own, slot_of(expert_ids, capacity).T, expert_gates.T),
        (query_weight, key_weight, value_weight, output_weight.T),
    )
    normed_all = normed_all.reshape(tok_rows, width_dim)
    *shard_rows, out_rows = [rows.reshape(width_dim, -1) for rows in shard_rows]
    q_lin, k_lin, v_lin = tuple(
        (
            jnp.dot(normed_all, weight_rows, preferred_element_type=jnp.float32)
            for weight_rows in shard_rows
        )
    )
    q_lin, k_lin = by_rows(q_lin), by_rows(k_lin)
    first_pos = lax.axis_index("seq") * tok_rows
    positions = (first_pos + jnp.arange(tok_rows, dtype=jnp.int32)).astype(jnp.float32)
    q_heads = q_cols // HD
    kv_heads = kv_cols // HD
    group_size = q_heads // kv_heads
    queries = (
        rotate(q_lin.reshape(tok_rows, q_heads, HD), positions)
        .astype(jnp.bfloat16)
        .reshape(tok_rows, kv_heads, group_size, HD)
    )
    keys_rot = (
        rotate(k_lin.reshape(tok_rows, kv_heads, HD), positions)
        .astype(jnp.bfloat16)
        .reshape(tok_rows, kv_cols)
    )
    values_cast = v_lin.astype(jnp.bfloat16)
    prev_keys, prev_values = passed_along(
        (keys_rot[tok_rows - WIN :], values_cast[tok_rows - WIN :]), "seq", 1
    )
    key_all = jnp.concatenate([prev_keys, keys_rot], axis=0).reshape(WIN + tok_rows, kv_heads, HD)
    val_all = jnp.concatenate([prev_values, values_cast], axis=0).reshape(
        WIN + tok_rows, kv_heads, HD
    )
    block_len = min(tok_rows, 512)
    sink_grid = sink_logits.reshape(kv_heads, group_size)

    def one_block(block):
        row_first = block * block_len
        return attend(queries, key_all, val_all, sink_grid, first_pos + row_first, WIN)

    attended = lax.map(one_block, jnp.arange(tok_rows // block_len, dtype=jnp.int32)).reshape(
        tok_rows, q_cols
    )
    head_partial = lax.dot_general(
        attended, out_rows, (((1,), (1,)), ((), ())), preferred_element_type=jnp.float32
    ).astype(jnp.bfloat16)
    head_sum = lax.psum_scatter(
        by_rows(head_partial), "ep", scatter_dimension=0, tiled=True
    ).astype(jnp.float32)
    mixed = act_f32 + head_sum
    mlp_in = normed(mixed, mlp_gain).astype(jnp.bfloat16)
    plane_rows = seq_count * capacity
    place = jnp.arange(plane_rows, dtype=jnp.int32)
    first_slots = (place // capacity * ep_count + lax.axis_index("ep")) * capacity
    plane_slots = first_slots + place % capacity
    picks = sum(
        (line_slots[:, k, None, :] == plane_slots[None, :, None]).astype(jnp.bfloat16)
        for k in range(top_k)
    )
    gate_at = sum(
        jnp.where(
            line_slots[:, k, :, None] == plane_slots[None, None, :],
            line_gates[:, k, :, None],
            0.0,
        )
        for k in range(top_k)
    )
    gate_parts = jnp.concatenate(three_parts(gate_at), axis=1)
    return mixture(
        mlp_in, picks, gate_parts, mixed, expert_in[0], expert_out[0], capacity
    )


def solution(mesh):
    return jax.shard_map(
        body,
        mesh=mesh,
        in_specs=(
            P(("seq", "ep"), None),
            P(),
            P("seq", "ep"),
            P("seq", "ep"),
            P("seq", "ep"),
            P("ep", "seq"),
            P("ep"),
            P(),
            P(("seq", "ep"), None),
            P(("seq", "ep"), None),
            P(("seq", "ep"), None, None),
            P(("seq", "ep"), None, None),
        ),
        out_specs=P(("seq", "ep"), None),
        check_vma=False,
    )
```

```python
import functools

import jax
import jax.numpy as jnp
from jax import lax
from jax.experimental import pallas as pl
from jax.experimental.layout import Layout, with_layout_constraint
from jax.experimental.pallas import tpu as pltpu
from jax.sharding import PartitionSpec as P

MESH = pl.DeviceIdType.MESH

HD = 64
WIN = 128


def passed_along(x, axis, by):
    count = lax.axis_size(axis)
    pairs = [(i, i + by) for i in range(count) if 0 <= i + by < count]
    return lax.ppermute(x, axis, pairs)


def normed(rows_f32, gain_vec):
    inv_rms = lax.rsqrt(jnp.mean(rows_f32 * rows_f32, axis=-1, keepdims=True) + 1e-05)
    return rows_f32 * inv_rms * gain_vec


def rotate(head_vals, positions):
    half_dim = head_vals.shape[-1] // 2
    inv_freq = 150000.0 ** (-jnp.arange(half_dim, dtype=jnp.float32) / half_dim)
    angles = positions[:, None] * inv_freq[None, :]
    cosines = jnp.cos(angles)[:, None, :]
    sines = jnp.sin(angles)[:, None, :]
    first = head_vals[..., :half_dim]
    second = head_vals[..., half_dim:]
    return jnp.concatenate(
        [first * cosines - second * sines, second * cosines + first * sines], axis=-1
    )


def attend(queries, key_rows, val_rows, sink_grid, query_first, win_len):
    scores = (
        jnp.einsum("qkgd,jkd->kgqj", queries, key_rows, preferred_element_type=jnp.float32) * 0.125
    )
    q_pos = query_first + jnp.arange(queries.shape[0], dtype=jnp.int32)
    k_pos = query_first - win_len + jnp.arange(key_rows.shape[0], dtype=jnp.int32)
    offset = q_pos[:, None] - k_pos[None, :]
    allowed = (offset >= 0) & (offset < win_len) & (k_pos[None, :] >= 0)
    scores = jnp.where(allowed, scores, jnp.float32(-1e30))
    peak_val = jnp.maximum(jnp.max(scores, axis=-1), sink_grid[:, :, None])
    exp_terms = jnp.exp(scores - peak_val[..., None])
    denominator = jnp.sum(exp_terms, axis=-1) + jnp.exp(sink_grid[:, :, None] - peak_val)
    weights = (exp_terms / denominator[..., None]).astype(jnp.bfloat16)
    mixed_vals = jnp.einsum("kgqj,jkd->qkgd", weights, val_rows, preferred_element_type=jnp.float32)
    return mixed_vals.astype(jnp.bfloat16)


def remote(src, dst, send_sem, recv_sem, device):
    return pltpu.make_async_remote_copy(
        src_ref=src,
        dst_ref=dst,
        send_sem=send_sem,
        recv_sem=recv_sem,
        device_id=device,
        device_id_type=MESH,
    )


def gather_kernel(n_seq, n_ep, n_line, n_plane, *refs):
    total = n_line + n_plane
    ins, outs, bufs = refs[:total], refs[total : 2 * total], refs[2 * total : 3 * total]
    own_sem, line_send, line_recv, plane_send, plane_recv, fwd_send, turn_send, turn_recv = refs[
        3 * total :
    ]
    seq, ep = lax.axis_index("seq"), lax.axis_index("ep")
    chips = n_seq // 2
    chip, core = seq // 2, seq % 2
    partner = chip * 2 + 1 - core

    barrier = pltpu.get_barrier_semaphore()

    @pl.when(ep > 0)
    def _():
        pl.semaphore_signal(barrier, inc=1, device_id=(seq, ep - 1), device_id_type=MESH)

    @pl.when(ep < n_ep - 1)
    def _():
        pl.semaphore_signal(barrier, inc=1, device_id=(seq, ep + 1), device_id_type=MESH)

    for d in range(1, chips):
        peer = lax.rem(chip + d, chips) * 2 + core
        pl.semaphore_signal(barrier, inc=1, device_id=(peer, ep), device_id_type=MESH)
    pl.semaphore_signal(barrier, inc=1, device_id=(partner, ep), device_id_type=MESH)
    neighbours = (ep > 0).astype(jnp.int32) + (ep < n_ep - 1).astype(jnp.int32)
    pl.semaphore_wait(barrier, chips + neighbours)

    def line_copies(step, which, act):
        for i in which:
            left_src, right_src = ep - step, ep + step

            @pl.when((left_src >= 0) & (ep < n_ep - 1))
            def _():
                src = ins[i] if step == 0 else outs[i].at[left_src]
                act(
                    remote(
                        src,
                        outs[i].at[left_src],
                        line_send.at[i, 0, step],
                        line_recv.at[i, left_src],
                        (seq, ep + 1),
                    )
                )

            @pl.when((right_src < n_ep) & (ep > 0))
            def _():
                src = ins[i] if step == 0 else outs[i].at[right_src]
                act(
                    remote(
                        src,
                        outs[i].at[right_src],
                        line_send.at[i, 1, step],
                        line_recv.at[i, right_src],
                        (seq, ep - 1),
                    )
                )

    def line_arrived(step, which):
        for i in which:
            for src in (ep - step, ep + step):

                @pl.when((src >= 0) & (src < n_ep))
                def _():
                    remote(
                        ins[i],
                        outs[i].at[src],
                        line_send.at[i, 0, 0],
                        line_recv.at[i, src],
                        (seq, ep),
                    ).wait_recv()

    square = chips == 4
    half = ins[n_line].shape[0] // 32 * 16
    if square:
        beside, above = chip + 1 - 2 * (chip % 2), lax.rem(chip + 2, 4)
        across = 3 - chip
        targets = {0: partner, 1: beside * 2 + core, 2: above * 2 + core}
    else:
        targets = {d: lax.rem(chip + d, chips) * 2 + core for d in range(1, chips)}
        targets[0] = partner
    peers = [d for d in targets if d != 0]

    def plane_copy(i, d):
        return remote(
            ins[n_line + i],
            outs[n_line + i].at[seq],
            plane_send.at[i, d],
            plane_recv.at[i, seq],
            (targets[d], ep),
        )

    def fwd_copy(i, d, src):
        whole = outs[n_line + i].at[src]
        return remote(whole, whole, fwd_send.at[i, d], plane_recv.at[i, src], (partner, ep))

    def turn_copy(i, d):
        src = targets[d]
        rows = ins[n_line + i].shape[0]
        part = pl.ds(0, half) if d == 1 else pl.ds(half, rows - half)
        piece = outs[n_line + i].at[src, part]
        arrival = plane_recv if d == 1 else turn_recv
        return remote(
            piece, piece, turn_send.at[i, d], arrival.at[i, src], (targets[3 - d], ep)
        )

    def plane_arrived(i, src):
        whole = outs[n_line + i].at[src]
        remote(whole, whole, plane_send.at[i, 0], plane_recv.at[i, src], (partner, ep)).wait_recv()

    def halves_arrived(i, src):
        rows = ins[n_line + i].shape[0]
        for part, arrival in ((pl.ds(0, half), plane_recv), (pl.ds(half, rows - half), turn_recv)):
            piece = outs[n_line + i].at[src, part]
            remote(piece, piece, plane_send.at[i, 0], arrival.at[i, src], (partner, ep)).wait_recv()

    def near_arrived(which):
        for i in which:
            for d in peers:
                plane_arrived(i, targets[d])
                if square:
                    turn_copy(i, d).start()
                fwd_copy(i, d, targets[d]).start()

    def across_arrived(which):
        if square:
            for i in which:
                halves_arrived(i, across * 2 + core)
                fwd_copy(i, 3, across * 2 + core).start()

    every = range(n_line)
    last = n_plane - 1
    line_copies(0, every, lambda c: c.start())
    for i in range(n_plane):
        for d in (*peers, 0):
            plane_copy(i, d).start()
    for i in range(total):
        pltpu.make_async_copy(ins[i], bufs[i], own_sem.at[i]).start()
    for i in range(total):
        pltpu.make_async_copy(ins[i], bufs[i], own_sem.at[i]).wait()
        mine = outs[i].at[ep if i < n_line else seq]
        pltpu.make_async_copy(bufs[i], mine, own_sem.at[i]).start()
    for step in range(1, n_ep - 1):
        line_arrived(step, every)
        line_copies(step, every, lambda c: c.start())
        if step == 1:
            near_arrived(range(last))
    near_arrived([last])
    across_arrived(range(n_plane))
    line_arrived(n_ep - 1, every)
    for i in range(n_plane):
        for other in range(chips):
            plane_arrived(i, other * 2 + 1 - core)
    for i in range(total):
        mine = outs[i].at[ep if i < n_line else seq]
        pltpu.make_async_copy(bufs[i], mine, own_sem.at[i]).wait()
    for step in range(n_ep - 1):
        line_copies(step, every, lambda c: c.wait_send())
    for i in range(n_plane):
        for d in (*peers, 0):
            plane_copy(i, d).wait_send()
        for d in peers:
            fwd_copy(i, d, targets[d]).wait_send()
            if square:
                turn_copy(i, d).wait_send()
        if square:
            fwd_copy(i, 3, across * 2 + core).wait_send()


def gathered(line, plane):
    n_seq, n_ep = lax.axis_size("seq"), lax.axis_size("ep")
    arrays = tuple(line) + tuple(plane)
    n_line, n_plane, chips = len(line), len(plane), n_seq // 2
    counts = [n_ep] * n_line + [n_seq] * n_plane
    anywhere = pl.BlockSpec(memory_space=pl.ANY)
    sem = pltpu.SemaphoreType.DMA
    return pl.pallas_call(
        functools.partial(gather_kernel, n_seq, n_ep, n_line, n_plane),
        out_shape=[jax.ShapeDtypeStruct((c,) + a.shape, a.dtype) for c, a in zip(counts, arrays)],
        in_specs=[anywhere] * len(arrays),
        out_specs=[anywhere] * len(arrays),
        scratch_shapes=[pltpu.VMEM(a.shape, a.dtype) for a in arrays]
        + [
            sem((len(arrays),)),
            sem((n_line, 2, n_ep)),
            sem((n_line, n_ep)),
            sem((n_plane, chips)),
            sem((n_plane, n_seq)),
            sem((n_plane, chips)),
            sem((n_plane, 3)),
            sem((n_plane, n_seq)),
        ],
        compiler_params=pltpu.CompilerParams(
            collective_id=0, has_side_effects=True, vmem_limit_bytes=16 << 20
        ),
        name="gather",
    )(*arrays)


def signal_all(barrier, n_seq, n_ep, seq, ep, line):
    for d in range(1, n_seq):
        pl.semaphore_signal(
            barrier, inc=1, device_id=(lax.rem(seq + d, n_seq), ep), device_id_type=MESH
        )
    count = jnp.int32(n_seq - 1)
    for d in line:
        there = (ep + d >= 0) & (ep + d < n_ep)

        @pl.when(there)
        def _():
            pl.semaphore_signal(barrier, inc=1, device_id=(seq, ep + d), device_id_type=MESH)

        count = count + there.astype(jnp.int32)
    pl.semaphore_wait(barrier, count)


def column_chunks(width, most=1024):
    return [(c, min(most, width - c)) for c in range(0, width, most)]


def pieces(width):
    return [(c, min(1024, width - c), min(1024, -(-width // 128) * 128 - c)) for c in range(0, width, 1024)]


def layer_kernel(
    n_seq,
    n_ep,
    cap,
    att_ref,
    wo_hbm,
    rows_ref,
    gain_ref,
    pick_ref,
    gate_ref,
    win_hbm,
    wout_hbm,
    out_ref,
    x_ref,
    held,
    parts,
    staged,
    arrived,
    back,
    sums,
    mine,
    taken,
    joined,
    act,
    w_in,
    w_out,
    weight_sem,
    wo_sem,
    head_send,
    head_recv,
    line_send,
    line_recv,
    send,
    recv,
    own,
    back_send,
    back_recv,
    back_own,
    sum_send,
    sum_recv,
):
    seq, ep = lax.axis_index("seq"), lax.axis_index("ep")
    rows, width = rows_ref.shape
    slots = n_seq * cap
    hidden = wout_hbm.shape[0]
    depth = att_ref.shape[1]
    cols = pieces(width)
    n_cols = len(cols)
    scale_at = x_ref.shape[1] - 128
    padded = back.shape[3]
    in_copy = pltpu.make_async_copy(win_hbm, w_in, weight_sem.at[0])
    out_copy = pltpu.make_async_copy(wout_hbm, w_out, weight_sem.at[1])

    def wo_place(i):
        return w_out.at[0 : cols[i][1], (i % 2) * depth : (i % 2 + 1) * depth]

    def wo_copy(i):
        c, size, _ = cols[i]
        return pltpu.make_async_copy(wo_hbm.at[pl.ds(c, size)], wo_place(i), wo_sem.at[i])

    for i in range(min(2, n_cols)):
        wo_copy(i).start()
    in_copy.start()
    signal_all(pltpu.get_barrier_semaphore(), n_seq, n_ep, seq, ep, (-1, 1))

    def spread(buffer, c, size, value):
        for s in range(n_seq):
            buffer[s, :, pl.ds(c, size)] = value[s * cap : (s + 1) * cap].astype(jnp.bfloat16)

    def together(buffer, c, size, first, count):
        slabs = [buffer[first + s, :, c : c + size].astype(jnp.float32) for s in range(count)]
        return jnp.concatenate(slabs, axis=0).astype(jnp.bfloat16)

    def relay(step, src, away, i, act_on):
        piece = pl.ds(i * 1024, 1024)

        @pl.when((src >= 0) & (src < n_ep) & (ep + away >= 0) & (ep + away < n_ep))
        def _():
            act_on(
                remote(
                    x_ref.at[:, piece] if step == 0 else held.at[src, :, piece],
                    held.at[src, :, piece],
                    line_send.at[(away + 1) // 2, step, i],
                    line_recv.at[src, i],
                    (seq, ep + away),
                )
            )

    def part(src, d, i):
        peer = lax.rem(seq + d, n_seq)
        piece = pl.ds(i * 1024, 1024)
        return remote(
            staged.at[src, peer, :, piece],
            arrived.at[src, seq, :, piece],
            send.at[src, d, i],
            recv.at[src, seq, i],
            (peer, ep),
        )

    def own_part(src, i):
        piece = pl.ds(i * 1024, 1024)
        return pltpu.make_async_copy(
            staged.at[src, seq, :, piece], arrived.at[src, seq, :, piece], own.at[src, i]
        )

    def back_part(src, d):
        peer = lax.rem(seq + d, n_seq)
        return remote(
            staged.at[src, peer, :, pl.ds(0, padded)],
            back.at[src, seq],
            back_send.at[src, d],
            back_recv.at[src, seq],
            (peer, ep),
        )

    def back_own_part(src):
        return pltpu.make_async_copy(
            staged.at[src, seq, :, pl.ds(0, padded)], back.at[src, seq], back_own.at[src]
        )

    def landing(at, step, way):
        return jnp.where(way == -1, n_ep, at) if step == 1 else at

    def line_sum(buffer, at, step, way, i, send_sem, recv_sem):
        c, _, size = cols[i]
        slot = landing(at, step, way)
        return remote(
            buffer.at[at, :, pl.ds(c, size)],
            sums.at[slot, :, pl.ds(c, size)],
            send_sem.at[at, i],
            recv_sem.at[slot, i],
            (seq, ep + way),
        )

    def head_copy(at, step, way, i):
        return line_sum(parts, at, step, way, i, head_send, head_recv)

    def sum_copy(at, step, way, i):
        return line_sum(held, at, step, way, i, sum_send, sum_recv)

    def sum_arrived(recv_sem, slot, i):
        c, _, size = cols[i]
        piece = sums.at[slot, :, pl.ds(c, size)]
        remote(piece, piece, sum_send.at[0, 0], recv_sem.at[slot, i], (seq, ep)).wait_recv()

    def each(d, act_on):
        at = ep + d

        @pl.when((at >= 0) & (at < n_ep))
        def _():
            act_on(at)

    def hand_out(src, from_ref, i):
        c = i * 1024
        picked = jnp.dot(
            pick_ref[src], from_ref[:, c : c + 1024], preferred_element_type=jnp.float32
        )
        spread(staged.at[src], c, 1024, picked)
        for d in range(1, n_seq):
            part(src, d, i).start()
        own_part(src, i).start()

    def expert(src):
        for i in range(n_cols):
            own_part(src, i).wait()
            for d in range(1, n_seq):
                peer = lax.rem(seq + d, n_seq)
                piece = arrived.at[src, peer, :, pl.ds(i * 1024, 1024)]
                remote(
                    piece, piece, send.at[src, 0, i], recv.at[src, peer, i], (peer, ep)
                ).wait_recv()

        group = n_seq if slots % 16 else 2
        for s in range(0, n_seq, group):
            taken[s * cap : (s + group) * cap, :] = together(
                arrived.at[src], 0, taken.shape[1], s, group
            )

        def up_columns(c, size):
            joined[:, pl.ds(c, size)] = jnp.dot(
                taken[:, 0:width], w_in[:, pl.ds(c, size)], preferred_element_type=jnp.float32
            )

        @pl.loop(0, width // 512)
        def _(i):
            up_columns(pl.multiple_of(i * 512, 512), 512)

        if width % 512:
            up_columns(width // 512 * 512, width % 512)

        @pl.loop(0, slots // 16)
        def _(i):
            r = pl.ds(pl.multiple_of(i * 16, 16), 16)
            scales = taken[r, scale_at : scale_at + 128].astype(jnp.float32)
            scale = jnp.sum(scales, axis=1, keepdims=True)
            gate = joined[r, 0:hidden] * scale
            up = joined[r, hidden : 2 * hidden] * scale
            act[r, :] = ((up + 1.0) * gate * jax.nn.sigmoid(1.702 * gate)).astype(jnp.bfloat16)

        for i in range(n_cols):
            for d in range(1, n_seq):
                part(src, d, i).wait_send()

        def down_columns(c, size):
            value = jnp.dot(
                act[...], w_out[:, pl.ds(c, size)], preferred_element_type=jnp.float32
            )
            spread(staged.at[src], c, size, value)

        @pl.loop(0, width // 512)
        def _(i):
            down_columns(pl.multiple_of(i * 512, 512), 512)

        if width % 512:
            down_columns(width // 512 * 512, width % 512)
        for d in range(1, n_seq):
            back_part(src, d).start()
        back_own_part(src).start()

    def gather_up(at, finish):
        back_own_part(at).wait()
        for d in range(1, n_seq):
            peer = lax.rem(seq + d, n_seq)
            piece = back.at[at, peer]
            remote(
                piece, piece, back_send.at[at, 0], back_recv.at[at, peer], (peer, ep)
            ).wait_recv()
        for i, (c, size, _) in enumerate(cols):
            results = together(back.at[at], c, size, 0, n_seq)
            three = jnp.dot(gate_ref[at], results, preferred_element_type=jnp.float32)
            finish(i, c, size, three[:rows] + three[rows : 2 * rows] + three[2 * rows :])

    def in_line(step, way, act_on):
        at = ep + way * step

        @pl.when((at >= 0) & (at < n_ep))
        def _():
            act_on(at)

    def pass_on(step, way):
        def one(at):
            for i in range(n_cols):
                relay(step, at, -way, i, lambda c: c.wait_send())

            def finish(i, c, size, value):
                before = ep - way
                joins = (before >= 0) & (before < n_ep)

                @pl.when(joins)
                def _():
                    sum_arrived(sum_recv, at, i)
                    sofar = sums[at, :, c : c + size].astype(jnp.float32)
                    held[at, :, c : c + size] = (value + sofar).astype(jnp.bfloat16)

                @pl.when(jnp.logical_not(joins))
                def _():
                    held[at, :, c : c + size] = value.astype(jnp.bfloat16)

                sum_copy(at, step, way, i).start()

            gather_up(at, finish)

        in_line(step, way, one)

    toward = jnp.where(2 * ep < n_ep, 1, -1)
    at_end = (ep == 0) | (ep == n_ep - 1)

    def project(i):
        c, size, _ = cols[i]
        wo_copy(i).wait()
        place = wo_place(i)

        def columns(first, count):
            value = lax.dot_general(
                att_ref[...],
                place[pl.ds(first, count), :],
                (((1,), (1,)), ((), ())),
                preferred_element_type=jnp.float32,
            ).astype(jnp.bfloat16)
            for at in range(n_ep):
                parts[at, :, pl.ds(c + first, count)] = value[at * rows : (at + 1) * rows]

        @pl.loop(0, size // 256)
        def _(j):
            columns(pl.multiple_of(j * 256, 256), 256)

        if size % 256:
            columns(size // 256 * 256, size % 256)
        if i + 2 < n_cols:
            wo_copy(i + 2).start()

    def head_on(step, way, i):
        c, size, _ = cols[i]

        def one(at):
            before = ep - way

            @pl.when((before >= 0) & (before < n_ep))
            def _():
                sum_arrived(head_recv, at, i)
                mixed = parts[at, :, c : c + size].astype(jnp.float32) + sums[
                    at, :, c : c + size
                ].astype(jnp.float32)
                parts[at, :, c : c + size] = mixed.astype(jnp.bfloat16)

            head_copy(at, step, way, i).start()

        in_line(step, way, one)

    def send_heads(i):
        for step in range(n_ep - 1, 0, -1):
            head_on(step, toward, i)
        for step in range(n_ep // 2 - 1, 0, -1):
            head_on(step, -toward, i)

    squares = []

    def own_rows(i):
        c, size, _ = cols[i]
        part_own = parts[ep, :, c : c + size].astype(jnp.float32)
        mine[:, c : c + size] = rows_ref[:, c : c + size].astype(jnp.float32) + part_own

        def add_from(slot):
            sum_arrived(head_recv, slot, i)
            mine[:, c : c + size] += sums[slot, :, c : c + size].astype(jnp.float32)

        @pl.when(ep > 0)
        def _():
            add_from(ep)

        @pl.when(ep < n_ep - 1)
        def _():
            add_from(n_ep)

        value = mine[:, c : c + size]
        squares.append(jnp.sum(value * value, axis=1, keepdims=True))
        x_ref[:, c : c + size] = (value * gain_ref[:, c : c + size]).astype(jnp.bfloat16)
        if i == n_cols - 1:
            scale = lax.rsqrt(sum(squares) / width + 1e-05)
            high = scale.astype(jnp.bfloat16).astype(jnp.float32)
            middle = (scale - high).astype(jnp.bfloat16).astype(jnp.float32)
            low = scale - high - middle
            lane = lax.broadcasted_iota(jnp.int32, (rows, 128), 1)
            tile = jnp.where(lane == 0, high, jnp.where(lane == 1, middle, 0.0))
            tile = jnp.where(lane == 2, low, tile)
            x_ref[:, scale_at : scale_at + 128] = tile.astype(jnp.bfloat16)
            gap = scale_at - width
            if gap:
                x_ref[:, width:scale_at] = jnp.zeros((rows, gap), jnp.bfloat16)
        for way in (1, -1):
            relay(0, ep, way, i, lambda c: c.start())
        hand_out(ep, x_ref, i)

    def from_line(step, i):
        for way in (1, -1):
            src = ep - way * step

            @pl.when((src >= 0) & (src < n_ep))
            def _():
                piece = held.at[src, :, pl.ds(i * 1024, 1024)]
                remote(
                    piece, piece, line_send.at[0, 0, 0], line_recv.at[src, i], (seq, ep)
                ).wait_recv()

            relay(step, src, way, i, lambda c: c.start())
        for way in (1, -1):
            each(-way * step, lambda at: hand_out(at, held.at[at], i))

    jobs = []
    for i in range(n_cols):
        jobs.append((3 * i - 1.5, 0, i))
        jobs.append((3 * i + 3, 1, i))
        for step in range(1, n_ep):
            jobs.append((3 * i + 3 + step, 2 + step, i))
    for _, kind, i in sorted(jobs):
        if kind == 0:
            project(i)
            send_heads(i)
            if i == n_cols - 1:
                out_copy.start()
        elif kind == 1:
            own_rows(i)
        else:
            from_line(kind - 2, i)
            if i == n_cols - 1:
                step = kind - 2
                if step == 1:
                    in_copy.wait()
                    out_copy.wait()
                    expert(ep)
                else:
                    for way in (1, -1):
                        each(-way * (step - 1), expert)

    @pl.when(at_end)
    def _():
        for step in range(1, n_ep - 2):
            pass_on(step, toward)

    for way in (1, -1):
        each(-way * (n_ep - 1), expert)

    @pl.when(jnp.logical_not(at_end))
    def _():
        for step in range(1, n_ep - 2):
            pass_on(step, toward)

    for step in range(max(1, n_ep - 2), n_ep):
        pass_on(step, toward)

    def keep(i, c, size, value):
        mine[:, c : c + size] += value

    gather_up(ep, keep)

    for step in range(1, n_ep // 2):
        pass_on(step, -toward)

    def add(slot):
        for i, (c, size, _) in enumerate(cols):
            sum_arrived(sum_recv, slot, i)
            mine[:, c : c + size] += sums[slot, :, c : c + size].astype(jnp.float32)

    @pl.when(ep > 0)
    def _():
        add(ep)

    @pl.when(ep < n_ep - 1)
    def _():
        add(n_ep)

    for c, size, _ in cols:
        out_ref[:, c : c + size] = mine[:, c : c + size].astype(jnp.bfloat16)
    for i in range(n_cols):
        for step in range(1, n_ep):
            for way in (1, -1):

                def sent(at):
                    head_copy(at, step, way, i).wait_send()
                    sum_copy(at, step, way, i).wait_send()

                each(way * step, sent)
        for way in (1, -1):
            relay(0, ep, way, i, lambda c: c.wait_send())
    for src in range(n_ep):
        for d in range(1, n_seq):
            back_part(src, d).wait_send()


def mixture(attended, out_rows, own, gain, picks, gates, w_in, w_out, cap):
    n_seq, n_ep = lax.axis_size("seq"), lax.axis_size("ep")
    rows, width = own.shape
    hidden = w_out.shape[0]
    slots = n_seq * cap
    n_cols = len(pieces(width))
    padded = -(-width // 128) * 128
    wide = n_cols * 1024
    if wide < padded + 128 or w_out.shape[0] < 1024 or width < 2 * attended.shape[1]:
        raise ValueError("unexpected widths")
    sem = pltpu.SemaphoreType.DMA
    vmem = pl.BlockSpec(memory_space=pltpu.VMEM)
    anywhere = pl.BlockSpec(memory_space=pl.ANY)
    return pl.pallas_call(
        functools.partial(layer_kernel, n_seq, n_ep, cap),
        out_shape=jax.ShapeDtypeStruct((rows, width), jnp.bfloat16),
        in_specs=[vmem, anywhere, vmem, vmem, vmem, vmem, anywhere, anywhere],
        out_specs=vmem,
        scratch_shapes=[
            pltpu.VMEM((rows, wide), jnp.bfloat16),
            pltpu.VMEM((n_ep, rows, wide), jnp.bfloat16),
            pltpu.VMEM((n_ep, rows, padded), jnp.bfloat16),
            pltpu.VMEM((n_ep, n_seq, cap, wide), jnp.bfloat16),
            pltpu.VMEM((n_ep, n_seq, cap, wide), jnp.bfloat16),
            pltpu.VMEM((n_ep, n_seq, cap, padded), jnp.bfloat16),
            pltpu.VMEM((n_ep + 1, rows, padded), jnp.bfloat16),
            pltpu.VMEM((rows, width), jnp.float32),
            pltpu.VMEM((slots, wide), jnp.bfloat16),
            pltpu.VMEM((slots, width), jnp.float32),
            pltpu.VMEM((slots, hidden), jnp.bfloat16),
            pltpu.VMEM(w_in.shape, jnp.bfloat16),
            pltpu.VMEM(w_out.shape, jnp.bfloat16),
            sem((2,)),
            sem((n_cols,)),
            sem((n_ep, n_cols)),
            sem((n_ep + 1, n_cols)),
            sem((2, n_ep, n_cols)),
            sem((n_ep, n_cols)),
            sem((n_ep, n_seq, n_cols)),
            sem((n_ep, n_seq, n_cols)),
            sem((n_ep, n_cols)),
            sem((n_ep, n_seq)),
            sem((n_ep, n_seq)),
            sem((n_ep,)),
            sem((n_ep, n_cols)),
            sem((n_ep + 1, n_cols)),
        ],
        compiler_params=pltpu.CompilerParams(
            collective_id=1, has_side_effects=True, vmem_limit_bytes=65200 << 10
        ),
        name="mixture",
    )(attended, out_rows, own, gain, picks, gates, w_in, w_out)


def slot_of(ids, capacity):
    count = ids.size
    flat = ids.reshape(-1)
    earlier = jnp.arange(count)[:, None] > jnp.arange(count)[None, :]
    same = (flat[:, None] == flat[None, :]) & earlier
    ranks = jnp.sum(same.astype(jnp.int32), axis=1)
    return (flat * capacity + ranks).reshape(ids.shape)


def three_parts(x):
    high = lax.reduce_precision(x, 8, 7)
    rest = x - high
    middle = lax.reduce_precision(rest, 8, 7)
    return high.astype(jnp.bfloat16), middle.astype(jnp.bfloat16), (rest - middle).astype(jnp.bfloat16)


def by_rows(x):
    return with_layout_constraint(x, Layout(tuple(range(x.ndim))))


def body(
    activations,
    attn_gain,
    query_weight,
    key_weight,
    value_weight,
    output_weight,
    sink_logits,
    mlp_gain,
    expert_ids,
    expert_gates,
    expert_in,
    expert_out,
):
    own_rows = activations.shape[0]
    width_dim = activations.shape[1]
    seq_count = lax.axis_size("seq")
    ep_count = lax.axis_size("ep")
    tok_rows = own_rows * ep_count
    act_f32 = activations.astype(jnp.float32)
    normed_own = normed(act_f32, attn_gain).astype(jnp.bfloat16)
    q_cols = query_weight.shape[1]
    kv_cols = key_weight.shape[1]
    experts_all = seq_count * ep_count
    top_k = expert_ids.shape[1]
    capacity = max(2, 3 * own_rows * top_k // (2 * experts_all))
    capacity = -(-capacity // 8) * 8
    (normed_all, line_slots, line_gates, *shard_rows) = gathered(
        (normed_own, slot_of(expert_ids, capacity).T, expert_gates.T),
        (query_weight, key_weight, value_weight, output_weight.T),
    )
    normed_all = normed_all.reshape(tok_rows, width_dim)
    *shard_rows, out_rows = [rows.reshape(width_dim, -1) for rows in shard_rows]
    q_lin, k_lin, v_lin = tuple(
        (
            jnp.dot(normed_all, weight_rows, preferred_element_type=jnp.float32)
            for weight_rows in shard_rows
        )
    )
    q_lin, k_lin = by_rows(q_lin), by_rows(k_lin)
    first_pos = lax.axis_index("seq") * tok_rows
    positions = (first_pos + jnp.arange(tok_rows, dtype=jnp.int32)).astype(jnp.float32)
    q_heads = q_cols // HD
    kv_heads = kv_cols // HD
    group_size = q_heads // kv_heads
    queries = (
        rotate(q_lin.reshape(tok_rows, q_heads, HD), positions)
        .astype(jnp.bfloat16)
        .reshape(tok_rows, kv_heads, group_size, HD)
    )
    keys_rot = (
        rotate(k_lin.reshape(tok_rows, kv_heads, HD), positions)
        .astype(jnp.bfloat16)
        .reshape(tok_rows, kv_cols)
    )
    values_cast = v_lin.astype(jnp.bfloat16)
    prev_keys, prev_values = passed_along(
        (keys_rot[tok_rows - WIN :], values_cast[tok_rows - WIN :]), "seq", 1
    )
    key_all = jnp.concatenate([prev_keys, keys_rot], axis=0).reshape(WIN + tok_rows, kv_heads, HD)
    val_all = jnp.concatenate([prev_values, values_cast], axis=0).reshape(
        WIN + tok_rows, kv_heads, HD
    )
    block_len = min(tok_rows, 512)
    sink_grid = sink_logits.reshape(kv_heads, group_size)

    def one_block(block):
        row_first = block * block_len
        return attend(queries, key_all, val_all, sink_grid, first_pos + row_first, WIN)

    attended = lax.map(one_block, jnp.arange(tok_rows // block_len, dtype=jnp.int32)).reshape(
        tok_rows, q_cols
    )
    plane_rows = seq_count * capacity
    place = jnp.arange(plane_rows, dtype=jnp.int32)
    first_slots = (place // capacity * ep_count + lax.axis_index("ep")) * capacity
    plane_slots = first_slots + place % capacity
    picks = sum(
        (line_slots[:, k, None, :] == plane_slots[None, :, None]).astype(jnp.bfloat16)
        for k in range(top_k)
    )
    gate_at = sum(
        jnp.where(
            line_slots[:, k, :, None] == plane_slots[None, None, :],
            line_gates[:, k, :, None],
            0.0,
        )
        for k in range(top_k)
    )
    gate_parts = jnp.concatenate(three_parts(gate_at), axis=1)
    return mixture(
        attended,
        out_rows,
        activations,
        mlp_gain[None, :],
        picks,
        gate_parts,
        expert_in[0],
        expert_out[0],
        capacity,
    )


def solution(mesh):
    return jax.shard_map(
        body,
        mesh=mesh,
        in_specs=(
            P(("seq", "ep"), None),
            P(),
            P("seq", "ep"),
            P("seq", "ep"),
            P("seq", "ep"),
            P("ep", "seq"),
            P("ep"),
            P(),
            P(("seq", "ep"), None),
            P(("seq", "ep"), None),
            P(("seq", "ep"), None, None),
            P(("seq", "ep"), None, None),
        ),
        out_specs=P(("seq", "ep"), None),
        check_vma=False,
    )
```

```python
import functools

import jax
import jax.numpy as jnp
from jax import lax
from jax.experimental import pallas as pl
from jax.experimental.layout import Layout, with_layout_constraint
from jax.experimental.pallas import tpu as pltpu
from jax.sharding import PartitionSpec as P

MESH = pl.DeviceIdType.MESH

HD = 64
WIN = 128


def passed_along(x, axis, by):
    count = lax.axis_size(axis)
    pairs = [(i, i + by) for i in range(count) if 0 <= i + by < count]
    return lax.ppermute(x, axis, pairs)


def normed(rows_f32, gain_vec):
    inv_rms = lax.rsqrt(jnp.mean(rows_f32 * rows_f32, axis=-1, keepdims=True) + 1e-05)
    return rows_f32 * inv_rms * gain_vec


def rotate(head_vals, positions):
    half_dim = head_vals.shape[1] // 2
    inv_freq = 150000.0 ** (-jnp.arange(half_dim, dtype=jnp.float32) / half_dim)
    angles = inv_freq[:, None] * positions[None, :]
    cosines = jnp.cos(angles)[None]
    sines = jnp.sin(angles)[None]
    first = head_vals[:, :half_dim]
    second = head_vals[:, half_dim:]
    return jnp.concatenate(
        [first * cosines - second * sines, second * cosines + first * sines], axis=1
    )


def attend_kernel(heads, q_ref, key_ref, val_ref, sink_ref, out_ref):
    tokens = q_ref.shape[1]
    first_pos = lax.axis_index("seq") * tokens
    groups = key_ref.shape[0] // HD
    lanes = heads * WIN

    @pl.loop(0, tokens // WIN)
    def _(block):
        start = pl.multiple_of(block * WIN, WIN)
        key_at = lax.broadcasted_iota(jnp.int32, (2 * WIN, WIN), 0)
        query_at = lax.broadcasted_iota(jnp.int32, (2 * WIN, WIN), 1)
        offset = WIN + query_at - key_at
        inside = first_pos + start - WIN + key_at >= 0
        allowed = (offset >= 0) & (offset < WIN) & inside
        barred = jnp.where(allowed, 0.0, jnp.float32(-1e30))
        for g in range(groups):
            first = g * heads * HD
            queries = jnp.concatenate(
                [
                    q_ref[first + h * HD : first + (h + 1) * HD, pl.ds(start, WIN)]
                    for h in range(heads)
                ],
                axis=1,
            )
            keys = key_ref[g * HD : (g + 1) * HD, pl.ds(start, 2 * WIN)]
            values = val_ref[g * HD : (g + 1) * HD, pl.ds(start, 2 * WIN)]
            scores = lax.dot_general(
                keys, queries, (((0,), (0,)), ((), ())), preferred_element_type=jnp.float32
            )
            bars = jnp.concatenate([barred] * heads, axis=1)
            scores = jnp.where(bars < 0.0, bars, scores * 0.125)
            sink = sink_ref[g : g + 1, :]
            peak = jnp.maximum(jnp.max(scores, axis=0, keepdims=True), sink)
            terms = jnp.exp(scores - peak)
            total = jnp.sum(terms, axis=0, keepdims=True) + jnp.exp(sink - peak)
            weights = (terms * (1.0 / total)).astype(jnp.bfloat16)
            mixed = jnp.dot(values, weights, preferred_element_type=jnp.float32)
            for h in range(0, heads, 2):
                pair = jnp.concatenate(
                    [mixed[:, h * WIN : (h + 1) * WIN], mixed[:, (h + 1) * WIN : (h + 2) * WIN]],
                    axis=0,
                )
                at = first + h * HD
                out_ref[pl.ds(start, WIN), at : at + 2 * HD] = pair.T.astype(jnp.bfloat16)


def attend(queries, keys, values, sinks, heads):
    cols, tokens = queries.shape
    vmem = pl.BlockSpec(memory_space=pltpu.VMEM)
    return pl.pallas_call(
        functools.partial(attend_kernel, heads),
        out_shape=jax.ShapeDtypeStruct((tokens, cols), jnp.bfloat16),
        in_specs=[vmem] * 4,
        out_specs=vmem,
        compiler_params=pltpu.CompilerParams(vmem_limit_bytes=24 << 20),
        cost_estimate=pl.CostEstimate(
            flops=8 * cols * tokens * WIN, bytes_accessed=4 * cols * tokens, transcendentals=0
        ),
        name="attend",
    )(queries, keys, values, jnp.repeat(sinks, WIN, axis=1))


def remote(src, dst, send_sem, recv_sem, device):
    return pltpu.make_async_remote_copy(
        src_ref=src,
        dst_ref=dst,
        send_sem=send_sem,
        recv_sem=recv_sem,
        device_id=device,
        device_id_type=MESH,
    )


def gather_kernel(n_seq, n_ep, n_line, n_plane, *refs):
    total = n_line + n_plane
    ins, outs, bufs = refs[:total], refs[total : 2 * total], refs[2 * total : 3 * total]
    own_sem, line_send, line_recv, plane_send, plane_recv, fwd_send, turn_send, turn_recv = refs[
        3 * total :
    ]
    seq, ep = lax.axis_index("seq"), lax.axis_index("ep")
    chips = n_seq // 2
    chip, core = seq // 2, seq % 2
    partner = chip * 2 + 1 - core

    barrier = pltpu.get_barrier_semaphore()

    @pl.when(ep > 0)
    def _():
        pl.semaphore_signal(barrier, inc=1, device_id=(seq, ep - 1), device_id_type=MESH)

    @pl.when(ep < n_ep - 1)
    def _():
        pl.semaphore_signal(barrier, inc=1, device_id=(seq, ep + 1), device_id_type=MESH)

    for d in range(1, chips):
        peer = lax.rem(chip + d, chips) * 2 + core
        pl.semaphore_signal(barrier, inc=1, device_id=(peer, ep), device_id_type=MESH)
    pl.semaphore_signal(barrier, inc=1, device_id=(partner, ep), device_id_type=MESH)
    neighbours = (ep > 0).astype(jnp.int32) + (ep < n_ep - 1).astype(jnp.int32)
    pl.semaphore_wait(barrier, chips + neighbours)

    def line_copies(step, which, act):
        for i in which:
            left_src, right_src = ep - step, ep + step

            @pl.when((left_src >= 0) & (ep < n_ep - 1))
            def _():
                src = ins[i] if step == 0 else outs[i].at[left_src]
                act(
                    remote(
                        src,
                        outs[i].at[left_src],
                        line_send.at[i, 0, step],
                        line_recv.at[i, left_src],
                        (seq, ep + 1),
                    )
                )

            @pl.when((right_src < n_ep) & (ep > 0))
            def _():
                src = ins[i] if step == 0 else outs[i].at[right_src]
                act(
                    remote(
                        src,
                        outs[i].at[right_src],
                        line_send.at[i, 1, step],
                        line_recv.at[i, right_src],
                        (seq, ep - 1),
                    )
                )

    def line_arrived(step, which):
        for i in which:
            for src in (ep - step, ep + step):

                @pl.when((src >= 0) & (src < n_ep))
                def _():
                    remote(
                        ins[i],
                        outs[i].at[src],
                        line_send.at[i, 0, 0],
                        line_recv.at[i, src],
                        (seq, ep),
                    ).wait_recv()

    square = chips == 4
    half = ins[n_line].shape[0] // 32 * 16
    if square:
        beside, above = chip + 1 - 2 * (chip % 2), lax.rem(chip + 2, 4)
        across = 3 - chip
        targets = {0: partner, 1: beside * 2 + core, 2: above * 2 + core}
    else:
        targets = {d: lax.rem(chip + d, chips) * 2 + core for d in range(1, chips)}
        targets[0] = partner
    peers = [d for d in targets if d != 0]

    def plane_copy(i, d):
        return remote(
            ins[n_line + i],
            outs[n_line + i].at[seq],
            plane_send.at[i, d],
            plane_recv.at[i, seq],
            (targets[d], ep),
        )

    def fwd_copy(i, d, src):
        whole = outs[n_line + i].at[src]
        return remote(whole, whole, fwd_send.at[i, d], plane_recv.at[i, src], (partner, ep))

    def turn_copy(i, d):
        src = targets[d]
        rows = ins[n_line + i].shape[0]
        part = pl.ds(0, half) if d == 1 else pl.ds(half, rows - half)
        piece = outs[n_line + i].at[src, part]
        arrival = plane_recv if d == 1 else turn_recv
        return remote(
            piece, piece, turn_send.at[i, d], arrival.at[i, src], (targets[3 - d], ep)
        )

    def plane_arrived(i, src):
        whole = outs[n_line + i].at[src]
        remote(whole, whole, plane_send.at[i, 0], plane_recv.at[i, src], (partner, ep)).wait_recv()

    def halves_arrived(i, src):
        rows = ins[n_line + i].shape[0]
        for part, arrival in ((pl.ds(0, half), plane_recv), (pl.ds(half, rows - half), turn_recv)):
            piece = outs[n_line + i].at[src, part]
            remote(piece, piece, plane_send.at[i, 0], arrival.at[i, src], (partner, ep)).wait_recv()

    def near_arrived(which):
        for i in which:
            for d in peers:
                plane_arrived(i, targets[d])
                if square:
                    turn_copy(i, d).start()
                fwd_copy(i, d, targets[d]).start()

    def across_arrived(which):
        if square:
            for i in which:
                halves_arrived(i, across * 2 + core)
                fwd_copy(i, 3, across * 2 + core).start()

    every = range(n_line)
    last = n_plane - 1
    line_copies(0, every, lambda c: c.start())
    for i in range(n_plane):
        for d in (*peers, 0):
            plane_copy(i, d).start()
    for i in range(total):
        pltpu.make_async_copy(ins[i], bufs[i], own_sem.at[i]).start()
    for i in range(total):
        pltpu.make_async_copy(ins[i], bufs[i], own_sem.at[i]).wait()
        mine = outs[i].at[ep if i < n_line else seq]
        pltpu.make_async_copy(bufs[i], mine, own_sem.at[i]).start()
    for step in range(1, n_ep - 1):
        line_arrived(step, every)
        line_copies(step, every, lambda c: c.start())
        if step == 1:
            near_arrived(range(last))
    near_arrived([last])
    across_arrived(range(n_plane))
    line_arrived(n_ep - 1, every)
    for i in range(n_plane):
        for other in range(chips):
            plane_arrived(i, other * 2 + 1 - core)
    for i in range(total):
        mine = outs[i].at[ep if i < n_line else seq]
        pltpu.make_async_copy(bufs[i], mine, own_sem.at[i]).wait()
    for step in range(n_ep - 1):
        line_copies(step, every, lambda c: c.wait_send())
    for i in range(n_plane):
        for d in (*peers, 0):
            plane_copy(i, d).wait_send()
        for d in peers:
            fwd_copy(i, d, targets[d]).wait_send()
            if square:
                turn_copy(i, d).wait_send()
        if square:
            fwd_copy(i, 3, across * 2 + core).wait_send()


def gathered(line, plane):
    n_seq, n_ep = lax.axis_size("seq"), lax.axis_size("ep")
    arrays = tuple(line) + tuple(plane)
    n_line, n_plane, chips = len(line), len(plane), n_seq // 2
    counts = [n_ep] * n_line + [n_seq] * n_plane
    anywhere = pl.BlockSpec(memory_space=pl.ANY)
    sem = pltpu.SemaphoreType.DMA
    return pl.pallas_call(
        functools.partial(gather_kernel, n_seq, n_ep, n_line, n_plane),
        out_shape=[jax.ShapeDtypeStruct((c,) + a.shape, a.dtype) for c, a in zip(counts, arrays)],
        in_specs=[anywhere] * len(arrays),
        out_specs=[anywhere] * len(arrays),
        scratch_shapes=[pltpu.VMEM(a.shape, a.dtype) for a in arrays]
        + [
            sem((len(arrays),)),
            sem((n_line, 2, n_ep)),
            sem((n_line, n_ep)),
            sem((n_plane, chips)),
            sem((n_plane, n_seq)),
            sem((n_plane, chips)),
            sem((n_plane, 3)),
            sem((n_plane, n_seq)),
        ],
        compiler_params=pltpu.CompilerParams(
            collective_id=0, has_side_effects=True, vmem_limit_bytes=60 << 20
        ),
        name="gather",
    )(*arrays)


def signal_all(barrier, n_seq, n_ep, seq, ep, line):
    for d in range(1, n_seq):
        pl.semaphore_signal(
            barrier, inc=1, device_id=(lax.rem(seq + d, n_seq), ep), device_id_type=MESH
        )
    count = jnp.int32(n_seq - 1)
    for d in line:
        there = (ep + d >= 0) & (ep + d < n_ep)

        @pl.when(there)
        def _():
            pl.semaphore_signal(barrier, inc=1, device_id=(seq, ep + d), device_id_type=MESH)

        count = count + there.astype(jnp.int32)
    pl.semaphore_wait(barrier, count)


def column_chunks(width, most=1024):
    return [(c, min(most, width - c)) for c in range(0, width, most)]


def pieces(width):
    return [(c, min(1024, width - c), min(1024, -(-width // 128) * 128 - c)) for c in range(0, width, 1024)]


def layer_kernel(
    n_seq,
    n_ep,
    cap,
    att_ref,
    wo_hbm,
    rows_ref,
    gain_ref,
    pick_ref,
    gate_ref,
    win_hbm,
    wout_hbm,
    out_ref,
    x_ref,
    held,
    parts,
    staged,
    arrived,
    back,
    sums,
    mine,
    taken,
    joined,
    act,
    w_in,
    w_out,
    weight_sem,
    wo_sem,
    head_send,
    head_recv,
    line_send,
    line_recv,
    send,
    recv,
    own,
    back_send,
    back_recv,
    back_own,
    sum_send,
    sum_recv,
):
    seq, ep = lax.axis_index("seq"), lax.axis_index("ep")
    rows, width = rows_ref.shape
    slots = n_seq * cap
    hidden = wout_hbm.shape[0]
    depth = att_ref.shape[1]
    cols = pieces(width)
    n_cols = len(cols)
    scale_at = x_ref.shape[1] - 128
    padded = back.shape[3]
    in_copy = pltpu.make_async_copy(win_hbm, w_in, weight_sem.at[0])
    out_copy = pltpu.make_async_copy(wout_hbm, w_out, weight_sem.at[1])

    def wo_place(i):
        return w_out.at[0 : cols[i][1], (i % 2) * depth : (i % 2 + 1) * depth]

    def wo_copy(i):
        c, size, _ = cols[i]
        return pltpu.make_async_copy(wo_hbm.at[pl.ds(c, size)], wo_place(i), wo_sem.at[i])

    for i in range(min(2, n_cols)):
        wo_copy(i).start()
    in_copy.start()
    signal_all(pltpu.get_barrier_semaphore(), n_seq, n_ep, seq, ep, (-1, 1))

    def spread(buffer, c, size, value):
        for s in range(n_seq):
            buffer[s, :, pl.ds(c, size)] = value[s * cap : (s + 1) * cap].astype(jnp.bfloat16)

    def together(buffer, c, size, first, count):
        slabs = [buffer[first + s, :, c : c + size].astype(jnp.float32) for s in range(count)]
        return jnp.concatenate(slabs, axis=0).astype(jnp.bfloat16)

    def relay(step, src, away, i, act_on):
        piece = pl.ds(i * 1024, 1024)

        @pl.when((src >= 0) & (src < n_ep) & (ep + away >= 0) & (ep + away < n_ep))
        def _():
            act_on(
                remote(
                    x_ref.at[:, piece] if step == 0 else held.at[src, :, piece],
                    held.at[src, :, piece],
                    line_send.at[(away + 1) // 2, step, i],
                    line_recv.at[src, i],
                    (seq, ep + away),
                )
            )

    def part(src, d, i):
        peer = lax.rem(seq + d, n_seq)
        piece = pl.ds(i * 1024, 1024)
        return remote(
            staged.at[src, peer, :, piece],
            arrived.at[src, seq, :, piece],
            send.at[src, d, i],
            recv.at[src, seq, i],
            (peer, ep),
        )

    def own_part(src, i):
        piece = pl.ds(i * 1024, 1024)
        return pltpu.make_async_copy(
            staged.at[src, seq, :, piece], arrived.at[src, seq, :, piece], own.at[src, i]
        )

    def back_part(src, d):
        peer = lax.rem(seq + d, n_seq)
        return remote(
            staged.at[src, peer, :, pl.ds(0, padded)],
            back.at[src, seq],
            back_send.at[src, d],
            back_recv.at[src, seq],
            (peer, ep),
        )

    def back_own_part(src):
        return pltpu.make_async_copy(
            staged.at[src, seq, :, pl.ds(0, padded)], back.at[src, seq], back_own.at[src]
        )

    def landing(at, step, way):
        return jnp.where(way == -1, n_ep, at) if step == 1 else at

    def line_sum(buffer, at, step, way, i, send_sem, recv_sem):
        c, _, size = cols[i]
        slot = landing(at, step, way)
        return remote(
            buffer.at[at, :, pl.ds(c, size)],
            sums.at[slot, :, pl.ds(c, size)],
            send_sem.at[at, i],
            recv_sem.at[slot, i],
            (seq, ep + way),
        )

    def head_copy(at, step, way, i):
        return line_sum(parts, at, step, way, i, head_send, head_recv)

    def sum_copy(at, step, way, i):
        return line_sum(held, at, step, way, i, sum_send, sum_recv)

    def sum_arrived(recv_sem, slot, i):
        c, _, size = cols[i]
        piece = sums.at[slot, :, pl.ds(c, size)]
        remote(piece, piece, sum_send.at[0, 0], recv_sem.at[slot, i], (seq, ep)).wait_recv()

    def each(d, act_on):
        at = ep + d

        @pl.when((at >= 0) & (at < n_ep))
        def _():
            act_on(at)

    def hand_out(src, from_ref, i):
        c = i * 1024
        picked = jnp.dot(
            pick_ref[src], from_ref[:, c : c + 1024], preferred_element_type=jnp.float32
        )
        spread(staged.at[src], c, 1024, picked)
        for d in range(1, n_seq):
            part(src, d, i).start()
        own_part(src, i).start()

    def expert(src):
        for i in range(n_cols):
            own_part(src, i).wait()
            for d in range(1, n_seq):
                peer = lax.rem(seq + d, n_seq)
                piece = arrived.at[src, peer, :, pl.ds(i * 1024, 1024)]
                remote(
                    piece, piece, send.at[src, 0, i], recv.at[src, peer, i], (peer, ep)
                ).wait_recv()

        group = n_seq if slots % 16 else 2
        for s in range(0, n_seq, group):
            taken[s * cap : (s + group) * cap, :] = together(
                arrived.at[src], 0, taken.shape[1], s, group
            )

        def up_columns(c, size):
            joined[:, pl.ds(c, size)] = jnp.dot(
                taken[:, 0:width], w_in[:, pl.ds(c, size)], preferred_element_type=jnp.float32
            )

        @pl.loop(0, width // 512)
        def _(i):
            up_columns(pl.multiple_of(i * 512, 512), 512)

        if width % 512:
            up_columns(width // 512 * 512, width % 512)

        @pl.loop(0, slots // 16)
        def _(i):
            r = pl.ds(pl.multiple_of(i * 16, 16), 16)
            scales = taken[r, scale_at : scale_at + 128].astype(jnp.float32)
            scale = jnp.sum(scales, axis=1, keepdims=True)
            gate = joined[r, 0:hidden] * scale
            up = joined[r, hidden : 2 * hidden] * scale
            act[r, :] = ((up + 1.0) * gate * jax.nn.sigmoid(1.702 * gate)).astype(jnp.bfloat16)

        for i in range(n_cols):
            for d in range(1, n_seq):
                part(src, d, i).wait_send()

        def down_columns(c, size):
            value = jnp.dot(
                act[...], w_out[:, pl.ds(c, size)], preferred_element_type=jnp.float32
            )
            spread(staged.at[src], c, size, value)

        @pl.loop(0, width // 512)
        def _(i):
            down_columns(pl.multiple_of(i * 512, 512), 512)

        if width % 512:
            down_columns(width // 512 * 512, width % 512)
        for d in range(1, n_seq):
            back_part(src, d).start()
        back_own_part(src).start()

    def gather_up(at, finish):
        back_own_part(at).wait()
        for d in range(1, n_seq):
            peer = lax.rem(seq + d, n_seq)
            piece = back.at[at, peer]
            remote(
                piece, piece, back_send.at[at, 0], back_recv.at[at, peer], (peer, ep)
            ).wait_recv()
        for i, (c, size, _) in enumerate(cols):
            results = together(back.at[at], c, size, 0, n_seq)
            three = jnp.dot(gate_ref[at], results, preferred_element_type=jnp.float32)
            finish(i, c, size, three[:rows] + three[rows : 2 * rows] + three[2 * rows :])

    def in_line(step, way, act_on):
        at = ep + way * step

        @pl.when((at >= 0) & (at < n_ep))
        def _():
            act_on(at)

    def pass_on(step, way):
        def one(at):
            for i in range(n_cols):
                relay(step, at, -way, i, lambda c: c.wait_send())

            def finish(i, c, size, value):
                before = ep - way
                joins = (before >= 0) & (before < n_ep)

                @pl.when(joins)
                def _():
                    sum_arrived(sum_recv, at, i)
                    sofar = sums[at, :, c : c + size].astype(jnp.float32)
                    held[at, :, c : c + size] = (value + sofar).astype(jnp.bfloat16)

                @pl.when(jnp.logical_not(joins))
                def _():
                    held[at, :, c : c + size] = value.astype(jnp.bfloat16)

                sum_copy(at, step, way, i).start()

            gather_up(at, finish)

        in_line(step, way, one)

    toward = jnp.where(2 * ep < n_ep, 1, -1)
    at_end = (ep == 0) | (ep == n_ep - 1)

    def project(i):
        c, size, _ = cols[i]
        wo_copy(i).wait()
        place = wo_place(i)

        def columns(first, count):
            value = lax.dot_general(
                att_ref[...],
                place[pl.ds(first, count), :],
                (((1,), (1,)), ((), ())),
                preferred_element_type=jnp.float32,
            ).astype(jnp.bfloat16)
            for at in range(n_ep):
                parts[at, :, pl.ds(c + first, count)] = value[at * rows : (at + 1) * rows]

        @pl.loop(0, size // 256)
        def _(j):
            columns(pl.multiple_of(j * 256, 256), 256)

        if size % 256:
            columns(size // 256 * 256, size % 256)
        if i + 2 < n_cols:
            wo_copy(i + 2).start()

    def head_on(step, way, i):
        c, size, _ = cols[i]

        def one(at):
            before = ep - way

            @pl.when((before >= 0) & (before < n_ep))
            def _():
                sum_arrived(head_recv, at, i)
                mixed = parts[at, :, c : c + size].astype(jnp.float32) + sums[
                    at, :, c : c + size
                ].astype(jnp.float32)
                parts[at, :, c : c + size] = mixed.astype(jnp.bfloat16)

            head_copy(at, step, way, i).start()

        in_line(step, way, one)

    def send_heads(i):
        for step in range(n_ep - 1, 0, -1):
            head_on(step, toward, i)
        for step in range(n_ep // 2 - 1, 0, -1):
            head_on(step, -toward, i)

    squares = []

    def own_rows(i):
        c, size, _ = cols[i]
        part_own = parts[ep, :, c : c + size].astype(jnp.float32)
        mine[:, c : c + size] = rows_ref[:, c : c + size].astype(jnp.float32) + part_own

        def add_from(slot):
            sum_arrived(head_recv, slot, i)
            mine[:, c : c + size] += sums[slot, :, c : c + size].astype(jnp.float32)

        @pl.when(ep > 0)
        def _():
            add_from(ep)

        @pl.when(ep < n_ep - 1)
        def _():
            add_from(n_ep)

        value = mine[:, c : c + size]
        squares.append(jnp.sum(value * value, axis=1, keepdims=True))
        x_ref[:, c : c + size] = (value * gain_ref[:, c : c + size]).astype(jnp.bfloat16)
        if i == n_cols - 1:
            scale = lax.rsqrt(sum(squares) / width + 1e-05)
            high = scale.astype(jnp.bfloat16).astype(jnp.float32)
            middle = (scale - high).astype(jnp.bfloat16).astype(jnp.float32)
            low = scale - high - middle
            lane = lax.broadcasted_iota(jnp.int32, (rows, 128), 1)
            tile = jnp.where(lane == 0, high, jnp.where(lane == 1, middle, 0.0))
            tile = jnp.where(lane == 2, low, tile)
            x_ref[:, scale_at : scale_at + 128] = tile.astype(jnp.bfloat16)
            gap = scale_at - width
            if gap:
                x_ref[:, width:scale_at] = jnp.zeros((rows, gap), jnp.bfloat16)
        for way in (1, -1):
            relay(0, ep, way, i, lambda c: c.start())
        hand_out(ep, x_ref, i)

    def from_line(step, i):
        for way in (1, -1):
            src = ep - way * step

            @pl.when((src >= 0) & (src < n_ep))
            def _():
                piece = held.at[src, :, pl.ds(i * 1024, 1024)]
                remote(
                    piece, piece, line_send.at[0, 0, 0], line_recv.at[src, i], (seq, ep)
                ).wait_recv()

            relay(step, src, way, i, lambda c: c.start())
        for way in (1, -1):
            each(-way * step, lambda at: hand_out(at, held.at[at], i))

    jobs = []
    for i in range(n_cols):
        jobs.append((3 * i - 1.5, 0, i))
        jobs.append((3 * i + 3, 1, i))
        for step in range(1, n_ep):
            jobs.append((3 * i + 3 + step, 2 + step, i))
    for _, kind, i in sorted(jobs):
        if kind == 0:
            project(i)
            send_heads(i)
            if i == n_cols - 1:
                out_copy.start()
        elif kind == 1:
            own_rows(i)
        else:
            from_line(kind - 2, i)
            if i == n_cols - 1:
                step = kind - 2
                if step == 1:
                    in_copy.wait()
                    out_copy.wait()
                    expert(ep)
                else:
                    for way in (1, -1):
                        each(-way * (step - 1), expert)

    @pl.when(at_end)
    def _():
        for step in range(1, n_ep - 2):
            pass_on(step, toward)

    for way in (1, -1):
        each(-way * (n_ep - 1), expert)

    @pl.when(jnp.logical_not(at_end))
    def _():
        for step in range(1, n_ep - 2):
            pass_on(step, toward)

    for step in range(max(1, n_ep - 2), n_ep):
        pass_on(step, toward)

    def keep(i, c, size, value):
        mine[:, c : c + size] += value

    gather_up(ep, keep)

    for step in range(1, n_ep // 2):
        pass_on(step, -toward)

    def add(slot):
        for i, (c, size, _) in enumerate(cols):
            sum_arrived(sum_recv, slot, i)
            mine[:, c : c + size] += sums[slot, :, c : c + size].astype(jnp.float32)

    @pl.when(ep > 0)
    def _():
        add(ep)

    @pl.when(ep < n_ep - 1)
    def _():
        add(n_ep)

    for c, size, _ in cols:
        out_ref[:, c : c + size] = mine[:, c : c + size].astype(jnp.bfloat16)
    for i in range(n_cols):
        for step in range(1, n_ep):
            for way in (1, -1):

                def sent(at):
                    head_copy(at, step, way, i).wait_send()
                    sum_copy(at, step, way, i).wait_send()

                each(way * step, sent)
        for way in (1, -1):
            relay(0, ep, way, i, lambda c: c.wait_send())
    for src in range(n_ep):
        for d in range(1, n_seq):
            back_part(src, d).wait_send()


def mixture(attended, out_rows, own, gain, picks, gates, w_in, w_out, cap):
    n_seq, n_ep = lax.axis_size("seq"), lax.axis_size("ep")
    rows, width = own.shape
    hidden = w_out.shape[0]
    slots = n_seq * cap
    n_cols = len(pieces(width))
    padded = -(-width // 128) * 128
    wide = n_cols * 1024
    if wide < padded + 128 or w_out.shape[0] < 1024 or width < 2 * attended.shape[1]:
        raise ValueError("unexpected widths")
    sem = pltpu.SemaphoreType.DMA
    vmem = pl.BlockSpec(memory_space=pltpu.VMEM)
    anywhere = pl.BlockSpec(memory_space=pl.ANY)
    return pl.pallas_call(
        functools.partial(layer_kernel, n_seq, n_ep, cap),
        out_shape=jax.ShapeDtypeStruct((rows, width), jnp.bfloat16),
        in_specs=[vmem, anywhere, vmem, vmem, vmem, vmem, anywhere, anywhere],
        out_specs=vmem,
        scratch_shapes=[
            pltpu.VMEM((rows, wide), jnp.bfloat16),
            pltpu.VMEM((n_ep, rows, wide), jnp.bfloat16),
            pltpu.VMEM((n_ep, rows, padded), jnp.bfloat16),
            pltpu.VMEM((n_ep, n_seq, cap, wide), jnp.bfloat16),
            pltpu.VMEM((n_ep, n_seq, cap, wide), jnp.bfloat16),
            pltpu.VMEM((n_ep, n_seq, cap, padded), jnp.bfloat16),
            pltpu.VMEM((n_ep + 1, rows, padded), jnp.bfloat16),
            pltpu.VMEM((rows, width), jnp.float32),
            pltpu.VMEM((slots, wide), jnp.bfloat16),
            pltpu.VMEM((slots, width), jnp.float32),
            pltpu.VMEM((slots, hidden), jnp.bfloat16),
            pltpu.VMEM(w_in.shape, jnp.bfloat16),
            pltpu.VMEM(w_out.shape, jnp.bfloat16),
            sem((2,)),
            sem((n_cols,)),
            sem((n_ep, n_cols)),
            sem((n_ep + 1, n_cols)),
            sem((2, n_ep, n_cols)),
            sem((n_ep, n_cols)),
            sem((n_ep, n_seq, n_cols)),
            sem((n_ep, n_seq, n_cols)),
            sem((n_ep, n_cols)),
            sem((n_ep, n_seq)),
            sem((n_ep, n_seq)),
            sem((n_ep,)),
            sem((n_ep, n_cols)),
            sem((n_ep + 1, n_cols)),
        ],
        compiler_params=pltpu.CompilerParams(
            collective_id=1, has_side_effects=True, vmem_limit_bytes=65200 << 10
        ),
        name="mixture",
    )(attended, out_rows, own, gain, picks, gates, w_in, w_out)


def slot_of(ids, capacity):
    count = ids.size
    flat = ids.reshape(-1)
    earlier = jnp.arange(count)[:, None] > jnp.arange(count)[None, :]
    same = (flat[:, None] == flat[None, :]) & earlier
    ranks = jnp.sum(same.astype(jnp.int32), axis=1)
    return (flat * capacity + ranks).reshape(ids.shape)


def three_parts(x):
    high = lax.reduce_precision(x, 8, 7)
    rest = x - high
    middle = lax.reduce_precision(rest, 8, 7)
    return high.astype(jnp.bfloat16), middle.astype(jnp.bfloat16), (rest - middle).astype(jnp.bfloat16)


def by_rows(x):
    return with_layout_constraint(x, Layout(tuple(range(x.ndim))))


def body(
    activations,
    attn_gain,
    query_weight,
    key_weight,
    value_weight,
    output_weight,
    sink_logits,
    mlp_gain,
    expert_ids,
    expert_gates,
    expert_in,
    expert_out,
):
    own_rows = activations.shape[0]
    width_dim = activations.shape[1]
    seq_count = lax.axis_size("seq")
    ep_count = lax.axis_size("ep")
    tok_rows = own_rows * ep_count
    act_f32 = activations.astype(jnp.float32)
    normed_own = normed(act_f32, attn_gain).astype(jnp.bfloat16)
    q_cols = query_weight.shape[1]
    kv_cols = key_weight.shape[1]
    experts_all = seq_count * ep_count
    top_k = expert_ids.shape[1]
    capacity = max(2, 3 * own_rows * top_k // (2 * experts_all))
    capacity = -(-capacity // 8) * 8
    (normed_all, line_slots, line_gates, *shard_rows) = gathered(
        (normed_own, slot_of(expert_ids, capacity).T, expert_gates.T),
        (query_weight, key_weight, value_weight, output_weight.T),
    )
    normed_all = normed_all.reshape(tok_rows, width_dim)
    *shard_rows, out_rows = [rows.reshape(width_dim, -1) for rows in shard_rows]

    def projected(weight_rows):
        return by_rows(jnp.dot(normed_all, weight_rows, preferred_element_type=jnp.float32)).T

    q_lin, k_lin, v_lin = [projected(weight_rows) for weight_rows in shard_rows]
    first_pos = lax.axis_index("seq") * tok_rows
    positions = (first_pos + jnp.arange(tok_rows, dtype=jnp.int32)).astype(jnp.float32)
    q_heads = q_cols // HD
    kv_heads = kv_cols // HD
    group_size = q_heads // kv_heads

    def rotated(lin):
        heads = lin.reshape(-1, HD, tok_rows)
        return rotate(heads, positions).astype(jnp.bfloat16).reshape(lin.shape)

    keys_values = jnp.concatenate([rotated(k_lin), v_lin.astype(jnp.bfloat16)], axis=0)
    before = passed_along(keys_values[:, tok_rows - WIN :], "seq", 1)
    keys_values = jnp.concatenate([before, keys_values], axis=1)
    attended = attend(
        rotated(q_lin),
        keys_values[:kv_cols],
        keys_values[kv_cols:],
        sink_logits.reshape(kv_heads, group_size),
        group_size,
    )
    plane_rows = seq_count * capacity
    place = jnp.arange(plane_rows, dtype=jnp.int32)
    first_slots = (place // capacity * ep_count + lax.axis_index("ep")) * capacity
    plane_slots = first_slots + place % capacity
    picks = sum(
        (line_slots[:, k, None, :] == plane_slots[None, :, None]).astype(jnp.bfloat16)
        for k in range(top_k)
    )
    gate_at = sum(
        jnp.where(
            line_slots[:, k, :, None] == plane_slots[None, None, :],
            line_gates[:, k, :, None],
            0.0,
        )
        for k in range(top_k)
    )
    gate_parts = jnp.concatenate(three_parts(gate_at), axis=1)
    return mixture(
        attended,
        out_rows,
        activations,
        mlp_gain[None, :],
        picks,
        gate_parts,
        expert_in[0],
        expert_out[0],
        capacity,
    )


def solution(mesh):
    return jax.shard_map(
        body,
        mesh=mesh,
        in_specs=(
            P(("seq", "ep"), None),
            P(),
            P("seq", "ep"),
            P("seq", "ep"),
            P("seq", "ep"),
            P("ep", "seq"),
            P("ep"),
            P(),
            P(("seq", "ep"), None),
            P(("seq", "ep"), None),
            P(("seq", "ep"), None, None),
            P(("seq", "ep"), None, None),
        ),
        out_specs=P(("seq", "ep"), None),
        check_vma=False,
    )
```

```python
import functools

import jax
import jax.numpy as jnp
from jax import lax
from jax.experimental import pallas as pl
from jax.experimental.layout import Layout, with_layout_constraint
from jax.experimental.pallas import tpu as pltpu
from jax.sharding import PartitionSpec as P

MESH = pl.DeviceIdType.MESH

HD = 64
WIN = 128
STEP = 768


def passed_along(x, axis, by):
    count = lax.axis_size(axis)
    pairs = [(i, i + by) for i in range(count) if 0 <= i + by < count]
    return lax.ppermute(x, axis, pairs)


def normed(rows_f32, gain_vec):
    inv_rms = lax.rsqrt(jnp.mean(rows_f32 * rows_f32, axis=-1, keepdims=True) + 1e-05)
    return rows_f32 * inv_rms * gain_vec


def rotate(head_vals, positions):
    half_dim = head_vals.shape[1] // 2
    inv_freq = 150000.0 ** (-jnp.arange(half_dim, dtype=jnp.float32) / half_dim)
    angles = inv_freq[:, None] * positions[None, :]
    cosines = jnp.cos(angles)[None]
    sines = jnp.sin(angles)[None]
    first = head_vals[:, :half_dim]
    second = head_vals[:, half_dim:]
    return jnp.concatenate(
        [first * cosines - second * sines, second * cosines + first * sines], axis=1
    )


def attend_kernel(heads, q_ref, key_ref, val_ref, sink_ref, out_ref):
    tokens = q_ref.shape[1]
    first_pos = lax.axis_index("seq") * tokens
    groups = key_ref.shape[0] // HD
    lanes = heads * WIN

    @pl.loop(0, tokens // WIN)
    def _(block):
        start = pl.multiple_of(block * WIN, WIN)
        key_at = lax.broadcasted_iota(jnp.int32, (2 * WIN, WIN), 0)
        query_at = lax.broadcasted_iota(jnp.int32, (2 * WIN, WIN), 1)
        offset = WIN + query_at - key_at
        inside = first_pos + start - WIN + key_at >= 0
        allowed = (offset >= 0) & (offset < WIN) & inside
        barred = jnp.where(allowed, 0.0, jnp.float32(-1e30))
        for g in range(groups):
            first = g * heads * HD
            queries = jnp.concatenate(
                [
                    q_ref[first + h * HD : first + (h + 1) * HD, pl.ds(start, WIN)]
                    for h in range(heads)
                ],
                axis=1,
            )
            keys = key_ref[g * HD : (g + 1) * HD, pl.ds(start, 2 * WIN)]
            values = val_ref[g * HD : (g + 1) * HD, pl.ds(start, 2 * WIN)]
            scores = lax.dot_general(
                keys, queries, (((0,), (0,)), ((), ())), preferred_element_type=jnp.float32
            )
            bars = jnp.concatenate([barred] * heads, axis=1)
            scores = jnp.where(bars < 0.0, bars, scores * 0.125)
            sink = sink_ref[g : g + 1, :]
            peak = jnp.maximum(jnp.max(scores, axis=0, keepdims=True), sink)
            terms = jnp.exp(scores - peak)
            total = jnp.sum(terms, axis=0, keepdims=True) + jnp.exp(sink - peak)
            weights = (terms * (1.0 / total)).astype(jnp.bfloat16)
            mixed = jnp.dot(values, weights, preferred_element_type=jnp.float32)
            for h in range(0, heads, 2):
                pair = jnp.concatenate(
                    [mixed[:, h * WIN : (h + 1) * WIN], mixed[:, (h + 1) * WIN : (h + 2) * WIN]],
                    axis=0,
                )
                at = first + h * HD
                out_ref[pl.ds(start, WIN), at : at + 2 * HD] = pair.T.astype(jnp.bfloat16)


def attend(queries, keys, values, sinks, heads):
    cols, tokens = queries.shape
    vmem = pl.BlockSpec(memory_space=pltpu.VMEM)
    return pl.pallas_call(
        functools.partial(attend_kernel, heads),
        out_shape=jax.ShapeDtypeStruct((tokens, cols), jnp.bfloat16),
        in_specs=[vmem] * 4,
        out_specs=vmem,
        compiler_params=pltpu.CompilerParams(vmem_limit_bytes=24 << 20),
        cost_estimate=pl.CostEstimate(
            flops=8 * cols * tokens * WIN, bytes_accessed=4 * cols * tokens, transcendentals=0
        ),
        name="attend",
    )(queries, keys, values, jnp.repeat(sinks, WIN, axis=1))


def remote(src, dst, send_sem, recv_sem, device):
    return pltpu.make_async_remote_copy(
        src_ref=src,
        dst_ref=dst,
        send_sem=send_sem,
        recv_sem=recv_sem,
        device_id=device,
        device_id_type=MESH,
    )


def gather_kernel(n_seq, n_ep, n_line, n_plane, *refs):
    total = n_line + n_plane
    ins, outs, bufs = refs[:total], refs[total : 2 * total], refs[2 * total : 3 * total]
    own_sem, line_send, line_recv, plane_send, plane_recv, fwd_send, turn_send, turn_recv = refs[
        3 * total :
    ]
    seq, ep = lax.axis_index("seq"), lax.axis_index("ep")
    chips = n_seq // 2
    chip, core = seq // 2, seq % 2
    partner = chip * 2 + 1 - core

    barrier = pltpu.get_barrier_semaphore()

    @pl.when(ep > 0)
    def _():
        pl.semaphore_signal(barrier, inc=1, device_id=(seq, ep - 1), device_id_type=MESH)

    @pl.when(ep < n_ep - 1)
    def _():
        pl.semaphore_signal(barrier, inc=1, device_id=(seq, ep + 1), device_id_type=MESH)

    for d in range(1, chips):
        peer = lax.rem(chip + d, chips) * 2 + core
        pl.semaphore_signal(barrier, inc=1, device_id=(peer, ep), device_id_type=MESH)
    pl.semaphore_signal(barrier, inc=1, device_id=(partner, ep), device_id_type=MESH)
    neighbours = (ep > 0).astype(jnp.int32) + (ep < n_ep - 1).astype(jnp.int32)
    pl.semaphore_wait(barrier, chips + neighbours)

    def line_copies(step, which, act):
        for i in which:
            left_src, right_src = ep - step, ep + step

            @pl.when((left_src >= 0) & (ep < n_ep - 1))
            def _():
                src = ins[i] if step == 0 else outs[i].at[left_src]
                act(
                    remote(
                        src,
                        outs[i].at[left_src],
                        line_send.at[i, 0, step],
                        line_recv.at[i, left_src],
                        (seq, ep + 1),
                    )
                )

            @pl.when((right_src < n_ep) & (ep > 0))
            def _():
                src = ins[i] if step == 0 else outs[i].at[right_src]
                act(
                    remote(
                        src,
                        outs[i].at[right_src],
                        line_send.at[i, 1, step],
                        line_recv.at[i, right_src],
                        (seq, ep - 1),
                    )
                )

    def line_arrived(step, which):
        for i in which:
            for src in (ep - step, ep + step):

                @pl.when((src >= 0) & (src < n_ep))
                def _():
                    remote(
                        ins[i],
                        outs[i].at[src],
                        line_send.at[i, 0, 0],
                        line_recv.at[i, src],
                        (seq, ep),
                    ).wait_recv()

    square = chips == 4
    half = ins[n_line].shape[0] // 32 * 16
    if square:
        beside, above = chip + 1 - 2 * (chip % 2), lax.rem(chip + 2, 4)
        across = 3 - chip
        targets = {0: partner, 1: beside * 2 + core, 2: above * 2 + core}
    else:
        targets = {d: lax.rem(chip + d, chips) * 2 + core for d in range(1, chips)}
        targets[0] = partner
    peers = [d for d in targets if d != 0]

    def plane_copy(i, d):
        return remote(
            ins[n_line + i],
            outs[n_line + i].at[seq],
            plane_send.at[i, d],
            plane_recv.at[i, seq],
            (targets[d], ep),
        )

    def fwd_copy(i, d, src):
        whole = outs[n_line + i].at[src]
        return remote(whole, whole, fwd_send.at[i, d], plane_recv.at[i, src], (partner, ep))

    def turn_copy(i, d):
        src = targets[d]
        rows = ins[n_line + i].shape[0]
        part = pl.ds(0, half) if d == 1 else pl.ds(half, rows - half)
        piece = outs[n_line + i].at[src, part]
        arrival = plane_recv if d == 1 else turn_recv
        return remote(
            piece, piece, turn_send.at[i, d], arrival.at[i, src], (targets[3 - d], ep)
        )

    def plane_arrived(i, src):
        whole = outs[n_line + i].at[src]
        remote(whole, whole, plane_send.at[i, 0], plane_recv.at[i, src], (partner, ep)).wait_recv()

    def halves_arrived(i, src):
        rows = ins[n_line + i].shape[0]
        for part, arrival in ((pl.ds(0, half), plane_recv), (pl.ds(half, rows - half), turn_recv)):
            piece = outs[n_line + i].at[src, part]
            remote(piece, piece, plane_send.at[i, 0], arrival.at[i, src], (partner, ep)).wait_recv()

    def near_arrived(which):
        for i in which:
            for d in peers:
                plane_arrived(i, targets[d])
                if square:
                    turn_copy(i, d).start()
                fwd_copy(i, d, targets[d]).start()

    def across_arrived(which):
        if square:
            for i in which:
                halves_arrived(i, across * 2 + core)
                fwd_copy(i, 3, across * 2 + core).start()

    every = range(n_line)
    last = n_plane - 1
    line_copies(0, every, lambda c: c.start())
    for i in range(n_plane):
        for d in (*peers, 0):
            plane_copy(i, d).start()
    for i in range(total):
        pltpu.make_async_copy(ins[i], bufs[i], own_sem.at[i]).start()
    for i in range(total):
        pltpu.make_async_copy(ins[i], bufs[i], own_sem.at[i]).wait()
        mine = outs[i].at[ep if i < n_line else seq]
        pltpu.make_async_copy(bufs[i], mine, own_sem.at[i]).start()
    for step in range(1, n_ep - 1):
        line_arrived(step, every)
        line_copies(step, every, lambda c: c.start())
        if step == 1:
            near_arrived(range(last))
    near_arrived([last])
    across_arrived(range(n_plane))
    line_arrived(n_ep - 1, every)
    for i in range(n_plane):
        for other in range(chips):
            plane_arrived(i, other * 2 + 1 - core)
    for i in range(total):
        mine = outs[i].at[ep if i < n_line else seq]
        pltpu.make_async_copy(bufs[i], mine, own_sem.at[i]).wait()
    for step in range(n_ep - 1):
        line_copies(step, every, lambda c: c.wait_send())
    for i in range(n_plane):
        for d in (*peers, 0):
            plane_copy(i, d).wait_send()
        for d in peers:
            fwd_copy(i, d, targets[d]).wait_send()
            if square:
                turn_copy(i, d).wait_send()
        if square:
            fwd_copy(i, 3, across * 2 + core).wait_send()


def gathered(line, plane):
    n_seq, n_ep = lax.axis_size("seq"), lax.axis_size("ep")
    arrays = tuple(line) + tuple(plane)
    n_line, n_plane, chips = len(line), len(plane), n_seq // 2
    counts = [n_ep] * n_line + [n_seq] * n_plane
    anywhere = pl.BlockSpec(memory_space=pl.ANY)
    sem = pltpu.SemaphoreType.DMA
    return pl.pallas_call(
        functools.partial(gather_kernel, n_seq, n_ep, n_line, n_plane),
        out_shape=[jax.ShapeDtypeStruct((c,) + a.shape, a.dtype) for c, a in zip(counts, arrays)],
        in_specs=[anywhere] * len(arrays),
        out_specs=[anywhere] * len(arrays),
        scratch_shapes=[pltpu.VMEM(a.shape, a.dtype) for a in arrays]
        + [
            sem((len(arrays),)),
            sem((n_line, 2, n_ep)),
            sem((n_line, n_ep)),
            sem((n_plane, chips)),
            sem((n_plane, n_seq)),
            sem((n_plane, chips)),
            sem((n_plane, 3)),
            sem((n_plane, n_seq)),
        ],
        compiler_params=pltpu.CompilerParams(
            collective_id=0, has_side_effects=True, vmem_limit_bytes=60 << 20
        ),
        name="gather",
    )(*arrays)


def signal_all(barrier, n_seq, n_ep, seq, ep, line):
    for d in range(1, n_seq):
        pl.semaphore_signal(
            barrier, inc=1, device_id=(lax.rem(seq + d, n_seq), ep), device_id_type=MESH
        )
    count = jnp.int32(n_seq - 1)
    for d in line:
        there = (ep + d >= 0) & (ep + d < n_ep)

        @pl.when(there)
        def _():
            pl.semaphore_signal(barrier, inc=1, device_id=(seq, ep + d), device_id_type=MESH)

        count = count + there.astype(jnp.int32)
    pl.semaphore_wait(barrier, count)


def column_chunks(width, most=1024):
    return [(c, min(most, width - c)) for c in range(0, width, most)]


def pieces(width):
    padded = -(-width // 128) * 128
    return [(c, min(STEP, width - c), min(STEP, padded - c)) for c in range(0, width, STEP)]


def layer_kernel(
    n_seq,
    n_ep,
    cap,
    att_ref,
    wo_hbm,
    rows_ref,
    gain_ref,
    pick_ref,
    gate_ref,
    win_hbm,
    wout_hbm,
    out_ref,
    x_ref,
    held,
    parts,
    staged,
    arrived,
    back,
    sums,
    mine,
    taken,
    joined,
    act,
    w_in,
    w_out,
    weight_sem,
    wo_sem,
    head_send,
    head_recv,
    line_send,
    line_recv,
    send,
    recv,
    own,
    back_send,
    back_recv,
    back_own,
    sum_send,
    sum_recv,
):
    seq, ep = lax.axis_index("seq"), lax.axis_index("ep")
    rows, width = rows_ref.shape
    slots = n_seq * cap
    hidden = wout_hbm.shape[0]
    depth = att_ref.shape[1]
    cols = pieces(width)
    n_cols = len(cols)
    scale_at = x_ref.shape[1] - 128
    padded = back.shape[3]
    in_copy = pltpu.make_async_copy(win_hbm, w_in, weight_sem.at[0])
    out_copy = pltpu.make_async_copy(wout_hbm, w_out, weight_sem.at[1])

    def wo_place(i):
        return w_out.at[0 : cols[i][1], (i % 2) * depth : (i % 2 + 1) * depth]

    def wo_copy(i):
        c, size, _ = cols[i]
        return pltpu.make_async_copy(wo_hbm.at[pl.ds(c, size)], wo_place(i), wo_sem.at[i])

    for i in range(min(2, n_cols)):
        wo_copy(i).start()
    in_copy.start()
    signal_all(pltpu.get_barrier_semaphore(), n_seq, n_ep, seq, ep, (-1, 1))

    def spread(buffer, c, size, value):
        for s in range(n_seq):
            buffer[s, :, pl.ds(c, size)] = value[s * cap : (s + 1) * cap].astype(jnp.bfloat16)

    def together(buffer, c, size, first, count):
        slabs = [buffer[first + s, :, c : c + size].astype(jnp.float32) for s in range(count)]
        return jnp.concatenate(slabs, axis=0).astype(jnp.bfloat16)

    def relay(step, src, away, i, act_on):
        piece = pl.ds(i * STEP, STEP)

        @pl.when((src >= 0) & (src < n_ep) & (ep + away >= 0) & (ep + away < n_ep))
        def _():
            act_on(
                remote(
                    x_ref.at[:, piece] if step == 0 else held.at[src, :, piece],
                    held.at[src, :, piece],
                    line_send.at[(away + 1) // 2, step, i],
                    line_recv.at[src, i],
                    (seq, ep + away),
                )
            )

    def part(src, d, i):
        peer = lax.rem(seq + d, n_seq)
        piece = pl.ds(i * STEP, STEP)
        return remote(
            staged.at[src, peer, :, piece],
            arrived.at[src, seq, :, piece],
            send.at[src, d, i],
            recv.at[src, seq, i],
            (peer, ep),
        )

    def own_part(src, i):
        piece = pl.ds(i * STEP, STEP)
        return pltpu.make_async_copy(
            staged.at[src, seq, :, piece], arrived.at[src, seq, :, piece], own.at[src, i]
        )

    def back_part(src, d):
        peer = lax.rem(seq + d, n_seq)
        return remote(
            staged.at[src, peer, :, pl.ds(0, padded)],
            back.at[src, seq],
            back_send.at[src, d],
            back_recv.at[src, seq],
            (peer, ep),
        )

    def back_own_part(src):
        return pltpu.make_async_copy(
            staged.at[src, seq, :, pl.ds(0, padded)], back.at[src, seq], back_own.at[src]
        )

    def landing(at, step, way):
        return jnp.where(way == -1, n_ep, at) if step == 1 else at

    def line_sum(buffer, at, step, way, i, send_sem, recv_sem):
        c, _, size = cols[i]
        slot = landing(at, step, way)
        return remote(
            buffer.at[at, :, pl.ds(c, size)],
            sums.at[slot, :, pl.ds(c, size)],
            send_sem.at[at, i],
            recv_sem.at[slot, i],
            (seq, ep + way),
        )

    def head_copy(at, step, way, i):
        return line_sum(parts, at, step, way, i, head_send, head_recv)

    def sum_copy(at, step, way, i):
        return line_sum(held, at, step, way, i, sum_send, sum_recv)

    def sum_arrived(recv_sem, slot, i):
        c, _, size = cols[i]
        piece = sums.at[slot, :, pl.ds(c, size)]
        remote(piece, piece, sum_send.at[0, 0], recv_sem.at[slot, i], (seq, ep)).wait_recv()

    def each(d, act_on):
        at = ep + d

        @pl.when((at >= 0) & (at < n_ep))
        def _():
            act_on(at)

    def hand_out(src, from_ref, i):
        c = i * STEP
        picked = jnp.dot(
            pick_ref[src], from_ref[:, c : c + STEP], preferred_element_type=jnp.float32
        )
        spread(staged.at[src], c, STEP, picked)
        for d in range(1, n_seq):
            part(src, d, i).start()
        own_part(src, i).start()

    def expert(src):
        for i in range(n_cols):
            own_part(src, i).wait()
            for d in range(1, n_seq):
                peer = lax.rem(seq + d, n_seq)
                piece = arrived.at[src, peer, :, pl.ds(i * STEP, STEP)]
                remote(
                    piece, piece, send.at[src, 0, i], recv.at[src, peer, i], (peer, ep)
                ).wait_recv()

        group = n_seq if slots % 16 else 2
        for s in range(0, n_seq, group):
            taken[s * cap : (s + group) * cap, :] = together(
                arrived.at[src], 0, taken.shape[1], s, group
            )

        def up_columns(c, size):
            joined[:, pl.ds(c, size)] = jnp.dot(
                taken[:, 0:width], w_in[:, pl.ds(c, size)], preferred_element_type=jnp.float32
            )

        @pl.loop(0, width // 512)
        def _(i):
            up_columns(pl.multiple_of(i * 512, 512), 512)

        if width % 512:
            up_columns(width // 512 * 512, width % 512)

        @pl.loop(0, slots // 16)
        def _(i):
            r = pl.ds(pl.multiple_of(i * 16, 16), 16)
            scales = taken[r, scale_at : scale_at + 128].astype(jnp.float32)
            scale = jnp.sum(scales, axis=1, keepdims=True)
            gate = joined[r, 0:hidden] * scale
            up = joined[r, hidden : 2 * hidden] * scale
            act[r, :] = ((up + 1.0) * gate * jax.nn.sigmoid(1.702 * gate)).astype(jnp.bfloat16)

        for i in range(n_cols):
            for d in range(1, n_seq):
                part(src, d, i).wait_send()

        def down_columns(c, size):
            value = jnp.dot(
                act[...], w_out[:, pl.ds(c, size)], preferred_element_type=jnp.float32
            )
            spread(staged.at[src], c, size, value)

        @pl.loop(0, width // 512)
        def _(i):
            down_columns(pl.multiple_of(i * 512, 512), 512)

        if width % 512:
            down_columns(width // 512 * 512, width % 512)
        for d in range(1, n_seq):
            back_part(src, d).start()
        back_own_part(src).start()

    def gather_up(at, finish):
        back_own_part(at).wait()
        for d in range(1, n_seq):
            peer = lax.rem(seq + d, n_seq)
            piece = back.at[at, peer]
            remote(
                piece, piece, back_send.at[at, 0], back_recv.at[at, peer], (peer, ep)
            ).wait_recv()
        for i, (c, size, _) in enumerate(cols):
            results = together(back.at[at], c, size, 0, n_seq)
            three = jnp.dot(gate_ref[at], results, preferred_element_type=jnp.float32)
            finish(i, c, size, three[:rows] + three[rows : 2 * rows] + three[2 * rows :])

    def in_line(step, way, act_on):
        at = ep + way * step

        @pl.when((at >= 0) & (at < n_ep))
        def _():
            act_on(at)

    def pass_on(step, way):
        def one(at):
            for i in range(n_cols):
                relay(step, at, -way, i, lambda c: c.wait_send())

            def finish(i, c, size, value):
                before = ep - way
                joins = (before >= 0) & (before < n_ep)

                @pl.when(joins)
                def _():
                    sum_arrived(sum_recv, at, i)
                    sofar = sums[at, :, c : c + size].astype(jnp.float32)
                    held[at, :, c : c + size] = (value + sofar).astype(jnp.bfloat16)

                @pl.when(jnp.logical_not(joins))
                def _():
                    held[at, :, c : c + size] = value.astype(jnp.bfloat16)

                sum_copy(at, step, way, i).start()

            gather_up(at, finish)

        in_line(step, way, one)

    toward = jnp.where(2 * ep < n_ep, 1, -1)
    at_end = (ep == 0) | (ep == n_ep - 1)

    def project(i):
        c, size, _ = cols[i]
        wo_copy(i).wait()
        place = wo_place(i)

        def columns(first, count):
            value = lax.dot_general(
                att_ref[...],
                place[pl.ds(first, count), :],
                (((1,), (1,)), ((), ())),
                preferred_element_type=jnp.float32,
            ).astype(jnp.bfloat16)
            for at in range(n_ep):
                parts[at, :, pl.ds(c + first, count)] = value[at * rows : (at + 1) * rows]

        @pl.loop(0, size // 256)
        def _(j):
            columns(pl.multiple_of(j * 256, 256), 256)

        if size % 256:
            columns(size // 256 * 256, size % 256)
        if i + 2 < n_cols:
            wo_copy(i + 2).start()

    def head_on(step, way, i):
        c, size, _ = cols[i]

        def one(at):
            before = ep - way

            @pl.when((before >= 0) & (before < n_ep))
            def _():
                sum_arrived(head_recv, at, i)
                mixed = parts[at, :, c : c + size].astype(jnp.float32) + sums[
                    at, :, c : c + size
                ].astype(jnp.float32)
                parts[at, :, c : c + size] = mixed.astype(jnp.bfloat16)

            head_copy(at, step, way, i).start()

        in_line(step, way, one)

    def send_heads(i):
        for step in range(n_ep - 1, 0, -1):
            head_on(step, toward, i)
        for step in range(n_ep // 2 - 1, 0, -1):
            head_on(step, -toward, i)

    squares = []

    def own_rows(i):
        c, size, _ = cols[i]
        part_own = parts[ep, :, c : c + size].astype(jnp.float32)
        mine[:, c : c + size] = rows_ref[:, c : c + size].astype(jnp.float32) + part_own

        def add_from(slot):
            sum_arrived(head_recv, slot, i)
            mine[:, c : c + size] += sums[slot, :, c : c + size].astype(jnp.float32)

        @pl.when(ep > 0)
        def _():
            add_from(ep)

        @pl.when(ep < n_ep - 1)
        def _():
            add_from(n_ep)

        value = mine[:, c : c + size]
        squares.append(jnp.sum(value * value, axis=1, keepdims=True))
        x_ref[:, c : c + size] = (value * gain_ref[:, c : c + size]).astype(jnp.bfloat16)
        if i == n_cols - 1:
            scale = lax.rsqrt(sum(squares) / width + 1e-05)
            high = scale.astype(jnp.bfloat16).astype(jnp.float32)
            middle = (scale - high).astype(jnp.bfloat16).astype(jnp.float32)
            low = scale - high - middle
            lane = lax.broadcasted_iota(jnp.int32, (rows, 128), 1)
            tile = jnp.where(lane == 0, high, jnp.where(lane == 1, middle, 0.0))
            tile = jnp.where(lane == 2, low, tile)
            x_ref[:, scale_at : scale_at + 128] = tile.astype(jnp.bfloat16)
            gap = scale_at - width
            if gap:
                x_ref[:, width:scale_at] = jnp.zeros((rows, gap), jnp.bfloat16)
        for way in (1, -1):
            relay(0, ep, way, i, lambda c: c.start())
        hand_out(ep, x_ref, i)

    def from_line(step, i):
        for way in (1, -1):
            src = ep - way * step

            @pl.when((src >= 0) & (src < n_ep))
            def _():
                piece = held.at[src, :, pl.ds(i * STEP, STEP)]
                remote(
                    piece, piece, line_send.at[0, 0, 0], line_recv.at[src, i], (seq, ep)
                ).wait_recv()

            relay(step, src, way, i, lambda c: c.start())
        for way in (1, -1):
            each(-way * step, lambda at: hand_out(at, held.at[at], i))

    jobs = []
    for i in range(n_cols):
        jobs.append((3 * i - 1.5, 0, i))
        jobs.append((3 * i + 3, 1, i))
        for step in range(1, n_ep):
            jobs.append((3 * i + 3 + step, 2 + step, i))
    for _, kind, i in sorted(jobs):
        if kind == 0:
            project(i)
            send_heads(i)
            if i == n_cols - 1:
                out_copy.start()
        elif kind == 1:
            own_rows(i)
        else:
            from_line(kind - 2, i)
            if i == n_cols - 1:
                step = kind - 2
                if step == 1:
                    in_copy.wait()
                    out_copy.wait()
                    expert(ep)
                else:
                    for way in (1, -1):
                        each(-way * (step - 1), expert)

    @pl.when(at_end)
    def _():
        for step in range(1, n_ep - 2):
            pass_on(step, toward)

    for way in (1, -1):
        each(-way * (n_ep - 1), expert)

    @pl.when(jnp.logical_not(at_end))
    def _():
        for step in range(1, n_ep - 2):
            pass_on(step, toward)

    for step in range(max(1, n_ep - 2), n_ep):
        pass_on(step, toward)

    def keep(i, c, size, value):
        mine[:, c : c + size] += value

    gather_up(ep, keep)

    for step in range(1, n_ep // 2):
        pass_on(step, -toward)

    def add(slot):
        for i, (c, size, _) in enumerate(cols):
            sum_arrived(sum_recv, slot, i)
            mine[:, c : c + size] += sums[slot, :, c : c + size].astype(jnp.float32)

    @pl.when(ep > 0)
    def _():
        add(ep)

    @pl.when(ep < n_ep - 1)
    def _():
        add(n_ep)

    for c, size, _ in cols:
        out_ref[:, c : c + size] = mine[:, c : c + size].astype(jnp.bfloat16)
    for i in range(n_cols):
        for step in range(1, n_ep):
            for way in (1, -1):

                def sent(at):
                    head_copy(at, step, way, i).wait_send()
                    sum_copy(at, step, way, i).wait_send()

                each(way * step, sent)
        for way in (1, -1):
            relay(0, ep, way, i, lambda c: c.wait_send())
    for src in range(n_ep):
        for d in range(1, n_seq):
            back_part(src, d).wait_send()


def mixture(attended, out_rows, own, gain, picks, gates, w_in, w_out, cap):
    n_seq, n_ep = lax.axis_size("seq"), lax.axis_size("ep")
    rows, width = own.shape
    hidden = w_out.shape[0]
    slots = n_seq * cap
    n_cols = len(pieces(width))
    padded = -(-width // 128) * 128
    wide = n_cols * STEP
    if wide < padded + 128 or w_out.shape[0] < STEP or width < 2 * attended.shape[1]:
        raise ValueError("unexpected widths")
    sem = pltpu.SemaphoreType.DMA
    vmem = pl.BlockSpec(memory_space=pltpu.VMEM)
    anywhere = pl.BlockSpec(memory_space=pl.ANY)
    return pl.pallas_call(
        functools.partial(layer_kernel, n_seq, n_ep, cap),
        out_shape=jax.ShapeDtypeStruct((rows, width), jnp.bfloat16),
        in_specs=[vmem, anywhere, vmem, vmem, vmem, vmem, anywhere, anywhere],
        out_specs=vmem,
        scratch_shapes=[
            pltpu.VMEM((rows, wide), jnp.bfloat16),
            pltpu.VMEM((n_ep, rows, wide), jnp.bfloat16),
            pltpu.VMEM((n_ep, rows, padded), jnp.bfloat16),
            pltpu.VMEM((n_ep, n_seq, cap, wide), jnp.bfloat16),
            pltpu.VMEM((n_ep, n_seq, cap, wide), jnp.bfloat16),
            pltpu.VMEM((n_ep, n_seq, cap, padded), jnp.bfloat16),
            pltpu.VMEM((n_ep + 1, rows, padded), jnp.bfloat16),
            pltpu.VMEM((rows, width), jnp.float32),
            pltpu.VMEM((slots, wide), jnp.bfloat16),
            pltpu.VMEM((slots, width), jnp.float32),
            pltpu.VMEM((slots, hidden), jnp.bfloat16),
            pltpu.VMEM(w_in.shape, jnp.bfloat16),
            pltpu.VMEM(w_out.shape, jnp.bfloat16),
            sem((2,)),
            sem((n_cols,)),
            sem((n_ep, n_cols)),
            sem((n_ep + 1, n_cols)),
            sem((2, n_ep, n_cols)),
            sem((n_ep, n_cols)),
            sem((n_ep, n_seq, n_cols)),
            sem((n_ep, n_seq, n_cols)),
            sem((n_ep, n_cols)),
            sem((n_ep, n_seq)),
            sem((n_ep, n_seq)),
            sem((n_ep,)),
            sem((n_ep, n_cols)),
            sem((n_ep + 1, n_cols)),
        ],
        compiler_params=pltpu.CompilerParams(
            collective_id=1, has_side_effects=True, vmem_limit_bytes=65200 << 10
        ),
        name="mixture",
    )(attended, out_rows, own, gain, picks, gates, w_in, w_out)


def slot_of(ids, capacity):
    count = ids.size
    flat = ids.reshape(-1)
    earlier = jnp.arange(count)[:, None] > jnp.arange(count)[None, :]
    same = (flat[:, None] == flat[None, :]) & earlier
    ranks = jnp.sum(same.astype(jnp.int32), axis=1)
    return (flat * capacity + ranks).reshape(ids.shape)


def three_parts(x):
    high = lax.reduce_precision(x, 8, 7)
    rest = x - high
    middle = lax.reduce_precision(rest, 8, 7)
    return high.astype(jnp.bfloat16), middle.astype(jnp.bfloat16), (rest - middle).astype(jnp.bfloat16)


def by_rows(x):
    return with_layout_constraint(x, Layout(tuple(range(x.ndim))))


def body(
    activations,
    attn_gain,
    query_weight,
    key_weight,
    value_weight,
    output_weight,
    sink_logits,
    mlp_gain,
    expert_ids,
    expert_gates,
    expert_in,
    expert_out,
):
    own_rows = activations.shape[0]
    width_dim = activations.shape[1]
    seq_count = lax.axis_size("seq")
    ep_count = lax.axis_size("ep")
    tok_rows = own_rows * ep_count
    act_f32 = activations.astype(jnp.float32)
    normed_own = normed(act_f32, attn_gain).astype(jnp.bfloat16)
    q_cols = query_weight.shape[1]
    kv_cols = key_weight.shape[1]
    experts_all = seq_count * ep_count
    top_k = expert_ids.shape[1]
    capacity = max(2, 3 * own_rows * top_k // (2 * experts_all))
    capacity = -(-capacity // 8) * 8
    (normed_all, line_slots, line_gates, *shard_rows) = gathered(
        (normed_own, slot_of(expert_ids, capacity).T, expert_gates.T),
        (query_weight, key_weight, value_weight, output_weight.T),
    )
    normed_all = normed_all.reshape(tok_rows, width_dim)
    *shard_rows, out_rows = [rows.reshape(width_dim, -1) for rows in shard_rows]

    def projected(weight_rows):
        return by_rows(jnp.dot(normed_all, weight_rows, preferred_element_type=jnp.float32)).T

    q_lin, k_lin, v_lin = [projected(weight_rows) for weight_rows in shard_rows]
    first_pos = lax.axis_index("seq") * tok_rows
    positions = (first_pos + jnp.arange(tok_rows, dtype=jnp.int32)).astype(jnp.float32)
    q_heads = q_cols // HD
    kv_heads = kv_cols // HD
    group_size = q_heads // kv_heads

    def rotated(lin):
        heads = lin.reshape(-1, HD, tok_rows)
        return rotate(heads, positions).astype(jnp.bfloat16).reshape(lin.shape)

    keys_values = jnp.concatenate([rotated(k_lin), v_lin.astype(jnp.bfloat16)], axis=0)
    before = passed_along(keys_values[:, tok_rows - WIN :], "seq", 1)
    keys_values = jnp.concatenate([before, keys_values], axis=1)
    attended = attend(
        rotated(q_lin),
        keys_values[:kv_cols],
        keys_values[kv_cols:],
        sink_logits.reshape(kv_heads, group_size),
        group_size,
    )
    plane_rows = seq_count * capacity
    place = jnp.arange(plane_rows, dtype=jnp.int32)
    first_slots = (place // capacity * ep_count + lax.axis_index("ep")) * capacity
    plane_slots = first_slots + place % capacity
    picks = sum(
        (line_slots[:, k, None, :] == plane_slots[None, :, None]).astype(jnp.bfloat16)
        for k in range(top_k)
    )
    gate_at = sum(
        jnp.where(
            line_slots[:, k, :, None] == plane_slots[None, None, :],
            line_gates[:, k, :, None],
            0.0,
        )
        for k in range(top_k)
    )
    gate_parts = jnp.concatenate(three_parts(gate_at), axis=1)
    return mixture(
        attended,
        out_rows,
        activations,
        mlp_gain[None, :],
        picks,
        gate_parts,
        expert_in[0],
        expert_out[0],
        capacity,
    )


def solution(mesh):
    return jax.shard_map(
        body,
        mesh=mesh,
        in_specs=(
            P(("seq", "ep"), None),
            P(),
            P("seq", "ep"),
            P("seq", "ep"),
            P("seq", "ep"),
            P("ep", "seq"),
            P("ep"),
            P(),
            P(("seq", "ep"), None),
            P(("seq", "ep"), None),
            P(("seq", "ep"), None, None),
            P(("seq", "ep"), None, None),
        ),
        out_specs=P(("seq", "ep"), None),
        check_vma=False,
    )
```
